32 devices in a mesh: wide: 16 (over z, y, core), shift: 2 (over x).
Axes of the slice: x: 2, y: 2, z: 4, core: 2. Of those that a mesh axis runs over, the one named last changes fastest.
Arguments:
- particles: bfloat16 [1024, 8448], P('wide'), may hold values from -64 to 64
- group_id: int32 [1024, 1], P('wide'), may hold values from 0 to 15; in each aligned block of 64 rows (0 to 63, 64 to 127, ...) at most 8 rows name the same one
- ctf_curves: float32 [16, 4224], P('wide'), may hold values from -1 to 1
- projections: bfloat16 [16, 8448], P('wide')
- inv_noise: float32 [4224], replicated, may hold values from 0.5 to 2
- shifts: int32 [64, 2], P('shift'), may hold values from -8 to 8
Outputs:
- insertion: float32 [16, 12672], P('wide')
- log_evidence: float32 [1024], P('wide')
The draws below stay inside these ranges and needn't reach their ends.
Inputs may be any that keep to these rules, and one draw needn't show every extreme that they name: `group_id`: at most 8 of the rows of one device name the same group, a bound that some block reaches.
All inputs are finite; a program needn't handle non-finite values.
Results may differ from the reference program's by a relative error of at most 0.0029.
Values may be sent and summed in bfloat16 or wider, within the bound.
A program may use at most 64 MiB of HBM per device.

```python
import math
import jax
import jax.numpy as jnp
import numpy as np
from jax import lax

COEFFS = 4224
NTRANS = 64
PART_DEV = 64
PARTICLES = 1024
GROUPS = 16
ORIENT = 16
CAPACITY = 8


def base_values(value_key, row_count, col_count):
    values = jnp.clip(jax.random.normal(value_key, (row_count, col_count), jnp.float32), -3.0, 3.0)
    return values


def draw_particles(key, part):
    base_key = jax.random.fold_in(key, 101)
    scale_key, value_key = jax.random.split(base_key, 2)
    row_scale = jnp.exp(jax.random.uniform(scale_key, (PARTICLES, 1), jnp.float32, math.log(0.1), math.log(1.0)))
    values = row_scale * base_values(value_key, PARTICLES, 2 * COEFFS)
    return values.astype(jnp.bfloat16)


def draw_projections(key, part):
    base_key = jax.random.fold_in(key, 202)
    value_key = jax.random.fold_in(base_key, 0)
    factor = 2.6 / math.sqrt(2.0 * COEFFS)
    values = base_values(value_key, ORIENT, 2 * COEFFS) * factor
    return values.astype(jnp.bfloat16)


def draw_inv_noise(key, part):
    noise_key = jax.random.fold_in(key, 303)
    return jnp.exp(jax.random.uniform(noise_key, (COEFFS,), jnp.float32, math.log(0.5), math.log(2.0)))


def touch_ends(values, own_key, low, top_value):
    spot = [jax.random.randint(jax.random.fold_in(own_key, axis), (), 0, length) for axis, length in enumerate(values.shape)]
    main_axis = values.shape.index(max(values.shape))
    neighbour = spot[:main_axis] + [(spot[main_axis] + 1) % values.shape[main_axis]] + spot[main_axis + 1:]
    return values.at[tuple(spot)].set(low).at[tuple(neighbour)].set(top_value)


def shard_levels(own_key, shape, cuts, low, high):
    factor_of, own = 1.0, jax.random.fold_in(own_key, 6)
    for dim, parts in cuts:
        draws = jnp.exp(jax.random.uniform(jax.random.fold_in(own, dim), (parts,), jnp.float32, low / len(cuts), high / len(cuts)))
        factor_of = factor_of * jnp.repeat(draws, shape[dim] // parts).reshape([-1 if axis == dim else 1 for axis in range(len(shape))])
    return factor_of


def shared_out(own_key, own, number, rows, number_of, top, reach, slope):
    ranking = jax.random.permutation(own_key, number_of)
    heavy_load, usual = portions_of(number_of, rows * top, reach, slope, True), portions_of(number_of, rows * top, reach, slope, False)
    places = jnp.arange(number_of)

    def named(lengths, offset_by):
        used = int((lengths > 0).sum())
        fixed = max(1, used // 4)
        shifted = fixed + (places - fixed + offset_by * (used - fixed)) % max(1, number_of - fixed)
        return jnp.zeros((number_of,), jnp.int32).at[ranking[jnp.where(places < fixed, places, shifted)]].set(jnp.asarray(lengths, jnp.int32))

    lengths = jnp.where(number % 4 == 0, named(heavy_load, number // 4), named(usual, number - number // 4 - 1))
    mixed = jax.random.permutation(jax.random.fold_in(own, 3), number_of)
    donor, receiver = mixed[0:number_of // 2 * 2:2], mixed[1:number_of // 2 * 2:2]
    margin = jnp.minimum(lengths[donor] - 1, reach - lengths[receiver]) // 2
    margin = jnp.where((donor == ranking[0]) | (receiver == ranking[0]) | (lengths[receiver] == 0), 0, jnp.maximum(margin, 0))
    shifted = jax.random.randint(jax.random.fold_in(own, 4), (number_of // 2,), 0, 1 << 20) % (margin + 1)
    lengths = lengths.at[donor].add(-shifted).at[receiver].add(shifted)
    members = jnp.searchsorted(jnp.cumsum(lengths), jnp.arange(rows * top), side="right").astype(jnp.int32)
    table = members.reshape(top, rows).T
    table = table[jax.random.permutation(jax.random.fold_in(own, 1), rows)]
    offset_by = jax.random.randint(jax.random.fold_in(own, 2), (rows, 1), 0, top)
    return jnp.take_along_axis(table, (jnp.arange(top)[None, :] + offset_by) % top, axis=1)


def portions_of(number_of, total, most, slope, full):
    portions = [(1 << 20) // math.isqrt(rank ** slope) + 1 for rank in range(1, number_of + 1)]
    largest = most if full else min(most, max(-(-total // number_of), total * portions[0] // sum(portions)))
    least = 1 if total - largest >= number_of - 1 else 0
    counts, surplus = [largest] + [least] * (number_of - 1), total - largest - least * (number_of - 1)
    while surplus > 0:
        movable = [i for i in range(1, number_of) if counts[i] < largest] or [i for i in range(1, number_of) if counts[i] < most]
        pool, left = sum([portions[i] for i in movable]), surplus
        for i in movable:
            addition = min(most - counts[i], max(1, left * portions[i] // pool), surplus)
            counts[i] = counts[i] + addition
            surplus = surplus - addition
    return np.array(counts)


def setup_inputs(seed: int = 0) -> dict:
    arg_keys = jax.random.split(jax.random.key(seed), 7)
    particles = draw_particles(jax.random.fold_in(arg_keys[6], 71), 0)
    group_id_keys = jax.random.split(jax.random.fold_in(arg_keys[1], 1), PARTICLES // PART_DEV)
    group_id_turns = jax.random.permutation(jax.random.fold_in(arg_keys[1], 3), PARTICLES // PART_DEV)
    group_id = jax.vmap(lambda own, number: shared_out(jax.random.fold_in(arg_keys[1], 2), own, number, PART_DEV, GROUPS, 1, CAPACITY, 2))(group_id_keys, group_id_turns).reshape((PARTICLES, 1))
    ctf_curves = jnp.clip(jax.random.uniform(arg_keys[2], (GROUPS, COEFFS), jnp.float32, -1.0, 1.0) * shard_levels(arg_keys[2], (GROUPS, COEFFS), ((0, 16),), -0.4, 0.0), -1.0, 1.0)
    projections = draw_projections(jax.random.fold_in(arg_keys[6], 71), 0)
    inv_noise = draw_inv_noise(jax.random.fold_in(arg_keys[6], 71), 0)
    shifts = touch_ends(jax.random.randint(arg_keys[5], (NTRANS, 2), -8, 9), jax.random.fold_in(arg_keys[5], 1), -8, 8).astype(jnp.int32)
    return {"particles": particles, "group_id": group_id, "ctf_curves": ctf_curves, "projections": projections, "inv_noise": inv_noise, "shifts": shifts}


TWO_PI_BOX = 2.0 * math.pi / 128.0


def shift_tables(shifts, coeffs):
    coeff_index = jnp.arange(coeffs, dtype=jnp.int32)
    freq_x = (coeff_index // 128).astype(jnp.float32)
    freq_y = (coeff_index % 128 - 64).astype(jnp.float32)
    move_x = shifts[:, 0].astype(jnp.float32)
    move_y = shifts[:, 1].astype(jnp.float32)
    phase_angle = TWO_PI_BOX * (move_x[:, None] * freq_x[None, :] + move_y[:, None] * freq_y[None, :])
    return jnp.cos(phase_angle), jnp.sin(phase_angle)


def rotate_slices(slab, cos_table, sin_table):
    coeffs = cos_table.shape[1]
    real_part = slab[:, :coeffs].astype(jnp.float32)[:, None, :]
    imag_part = slab[:, coeffs:].astype(jnp.float32)[:, None, :]
    rot_real = real_part * cos_table[None] + imag_part * sin_table[None]
    rot_imag = imag_part * cos_table[None] - real_part * sin_table[None]
    joined = jnp.concatenate([rot_real, rot_imag], 2)
    return joined.reshape(slab.shape[0] * cos_table.shape[0], 2 * coeffs).astype(jnp.bfloat16)


def reference(particles, group_id, ctf_curves, projections, inv_noise, shifts):
    groups = group_id[:, 0].astype(jnp.int32)
    ctf_row = ctf_curves[groups]
    real_part = particles[:, :COEFFS].astype(jnp.float32)
    imag_part = particles[:, COEFFS:].astype(jnp.float32)
    noise_ctf = inv_noise[None, :] * ctf_row
    weighted = jnp.concatenate([noise_ctf * real_part, noise_ctf * imag_part], 1).astype(jnp.bfloat16)
    filtered = jnp.concatenate([ctf_row * real_part, ctf_row * imag_part], 1).astype(jnp.bfloat16)
    cos_table, sin_table = shift_tables(shifts, COEFFS)
    rotated = rotate_slices(projections, cos_table, sin_table)
    cross_term = jnp.dot(weighted, rotated.T, preferred_element_type=jnp.float32)
    slice_real = projections[:, :COEFFS].astype(jnp.float32)
    slice_imag = projections[:, COEFFS:].astype(jnp.float32)
    slice_power = slice_real * slice_real + slice_imag * slice_imag
    weight_sq = ctf_row * ctf_row * inv_noise[None, :]
    self_term = 0.5 * jnp.dot(weight_sq, slice_power.T, precision=lax.Precision.HIGHEST)
    scores = cross_term.reshape(PARTICLES, ORIENT, NTRANS) - self_term[:, :, None]
    row_max = jnp.max(scores, axis=(1, 2))
    exp_scores = jnp.exp(scores - row_max[:, None, None])
    row_total = jnp.sum(exp_scores, axis=(1, 2))
    weights = (exp_scores / row_total[:, None, None]).astype(jnp.bfloat16)
    log_evidence = row_max + jnp.log(row_total)
    flat_weights = weights.reshape(PARTICLES, ORIENT * NTRANS)
    update = jnp.dot(flat_weights.T, filtered, preferred_element_type=jnp.float32)
    update = update.reshape(ORIENT, NTRANS, 2 * COEFFS)
    upd_real = update[:, :, :COEFFS]
    upd_imag = update[:, :, COEFFS:]
    data_real = jnp.sum(upd_real * cos_table[None] - upd_imag * sin_table[None], 1)
    data_imag = jnp.sum(upd_real * sin_table[None] + upd_imag * cos_table[None], 1)
    weight_sum = jnp.sum(weights.astype(jnp.float32), 2)
    weight_data = jnp.dot(weight_sum.T, ctf_row * ctf_row, precision=lax.Precision.HIGHEST)
    insertion = jnp.concatenate([data_real, data_imag, weight_data], 1)
    return insertion, log_evidence
```

```python
import functools
import math

import jax
import jax.numpy as jnp
from jax import lax
from jax.experimental import pallas as pl
from jax.experimental.pallas import tpu as pltpu
from jax.sharding import PartitionSpec as P

LANE = 128
REACH = 8
NR = 2 * REACH + 1
PARTS = 3
STEP = 2.0 * math.pi / 128.0
HIGH = lax.Precision.HIGHEST
MESH = pl.DeviceIdType.MESH
F32 = jnp.float32
BF16 = jnp.bfloat16
NT_DIMS = (((1,), (1,)), ((), ()))
NN_DIMS = (((1,), (0,)), ((), ()))
TN_DIMS = (((0,), (0,)), ((), ()))


def dot(a, b, dims=NN_DIMS, precision=None):
    return lax.dot_general(a, b, dims, precision=precision, preferred_element_type=F32)


def turn(m):
    x = m - 128.0 * jnp.floor(m * (1.0 / 128.0) + 0.5)
    z = (32.0 - jnp.abs(x)) * STEP
    y = z * z
    p = 1.0 / 362880.0 - y * (1.0 / 39916800.0)
    p = -1.0 / 5040.0 + y * p
    p = 1.0 / 120.0 + y * p
    p = -1.0 / 6.0 + y * p
    return z + z * (y * p)


def cuts(L):
    n = min(PARTS, L)
    return [(L * c // n, L * (c + 1) // n) for c in range(n)]


def padded(n, m):
    return -(-n // m) * m


def kernel(
    cfg, x_hbm, gid_hbm, ctf_ref, proj_ref, noise_ref, sh_ref,
    out_ref, ev_ref,
    gid_ref, xbuf, cbuf, pbuf, shbuf, prow, nbuf, cos_t, sin_t, wgt, fil, evb, wsq, power, selfc, selfr, selft, rowbuf,
    sc, scr, tot, at, cs, w2, part, r1, stage, snd, r2, fbuf, obuf,
    x_sem, own_sem, ag_ssem, ag_rsem, mt_rsem, sh_ssem, sh_rsem,
    sc_ssem, sf_ssem, sc_rsem, r1_ssem, r1_rsem, r2_ssem, r2_rsem, f_ssem, f_rsem, o_sem,
):
    W, S, nl, L, NTL, R = cfg
    C = L * LANE
    NT = NTL * S
    H = W // 2
    NC = W // 2
    QB = 2
    NB = H // QB
    RB = QB * NT
    w = lax.axis_index("wide")
    s = lax.axis_index("shift")
    core = lax.rem(w, 2)
    chip = lax.div(w, 2)
    mate = chip * 2 + (1 - core)
    first = jnp.minimum(s * L, nl - L)
    start = pl.multiple_of(first * LANE, LANE)
    full = nl * LANE
    G = padded(W, LANE)
    window = pl.ds(start, C)

    def chip_at(k):
        return lax.rem(chip + k, NC)

    def remote(src, dst, ssem, rsem, wide=None, shift=None):
        return pltpu.make_async_remote_copy(
            src_ref=src, dst_ref=dst, send_sem=ssem, recv_sem=rsem,
            device_id=(w if wide is None else wide, s if shift is None else shift),
            device_id_type=MESH,
        )

    def settle(ref, sem):
        pltpu.make_async_copy(ref, ref, sem).wait()

    x_copies = [
        pltpu.make_async_copy(
            x_hbm.at[:, pl.ds(pl.multiple_of(start + h * full, LANE), C)],
            xbuf.at[h], x_sem,
        )
        for h in range(2)
    ]
    own = [
        pltpu.make_async_copy(ctf_ref.at[:, window], cbuf.at[w], own_sem.at[0]),
        pltpu.make_async_copy(proj_ref, prow, own_sem.at[1]),
        pltpu.make_async_copy(sh_ref, shbuf.at[s], own_sem.at[2]),
        pltpu.make_async_copy(noise_ref, nbuf.at[0], own_sem.at[3]),
        pltpu.make_async_copy(gid_hbm, gid_ref, own_sem.at[4]),
    ]
    for c in own + x_copies:
        c.start()

    bar = pltpu.get_barrier_semaphore()
    pl.semaphore_signal(bar, inc=1, device_id=(mate, s), device_id_type=MESH)

    def greet(k, carry):
        pl.semaphore_signal(
            bar, inc=1, device_id=(chip_at(k) * 2 + core, s), device_id_type=MESH
        )
        return carry

    lax.fori_loop(1, NC, greet, 0)
    for d in range(1, S):
        pl.semaphore_signal(
            bar, inc=1, device_id=(w, lax.rem(s + d, S)), device_id_type=MESH
        )
    own[1].wait()
    for h in range(2):
        pbuf[w, h : h + 1, :] = prow[:, pl.ds(pl.multiple_of(start + h * full, LANE), C)]

    pl.semaphore_wait(bar, NC + S - 1)

    def ag_pair(to, rsem):
        return (
            remote(ctf_ref.at[:, window], cbuf.at[w], ag_ssem.at[0], rsem, wide=to),
            remote(pbuf.at[w], pbuf.at[w], ag_ssem.at[1], rsem, wide=to),
        )

    def relay_pair(src):
        return (
            remote(cbuf.at[src], cbuf.at[src], ag_ssem.at[0], mt_rsem, wide=mate),
            remote(pbuf.at[src], pbuf.at[src], ag_ssem.at[1], mt_rsem, wide=mate),
        )

    sh_copies = [
        remote(sh_ref, shbuf.at[s], sh_ssem, sh_rsem, shift=lax.rem(s + d, S))
        for d in range(1, S)
    ]
    for c in sh_copies:
        c.start()

    def ag_start(k, carry):
        for c in ag_pair(chip_at(k) * 2 + core, ag_rsem.at[chip]):
            c.start()
        return carry

    lax.fori_loop(1, NC, ag_start, 0)
    for c in ag_pair(mate, mt_rsem):
        c.start()

    for c in own[:1] + own[2:]:
        c.wait()
    settle(shbuf.at[: S - 1], sh_rsem)

    lane = lax.broadcasted_iota(jnp.int32, (2, 2 * LANE), 1)
    axis = lax.broadcasted_iota(jnp.int32, (2, 2 * LANE), 0)
    freq = jnp.where(
        lane < LANE, jnp.where(axis == 0, first + lane, 0), jnp.where(axis == 1, lane - LANE - 64, 0)
    ).astype(F32)
    ang = STEP * jnp.concatenate(
        [dot(shbuf[t].astype(F32), freq, TN_DIMS, HIGH) for t in range(S)], axis=0
    )
    ang_a, ang_b = ang[:, :LANE], ang[:, LANE:]
    kx = first + lax.broadcasted_iota(jnp.int32, (NT, LANE), 1)
    live = jnp.where(kx >= s * L, 1.0, 0.0)
    cos_b, sin_b = jnp.cos(ang_b), jnp.sin(ang_b)
    cos_a, sin_a = jnp.cos(ang_a) * live, jnp.sin(ang_a) * live
    for l in range(L):
        ca, sa = cos_a[:, l : l + 1], sin_a[:, l : l + 1]
        cols = pl.ds(l * LANE, LANE)
        cos_t[:, cols] = ca * cos_b - sa * sin_b
        sin_t[:, cols] = sa * cos_b + ca * sin_b

    qn = at.shape[0]
    q = lax.broadcasted_iota(jnp.int32, (qn, 2 * NT), 0).astype(F32)
    lanes = lax.broadcasted_iota(jnp.int32, (qn, 2 * NT), 1)
    line = jnp.floor((q + 0.5) * (1.0 / NR))
    kind = q - line * NR
    sx, sy = (
        jnp.concatenate([shbuf[t][a : a + 1, :] for t in range(S)] * 2, axis=1).astype(F32)
        for a in range(2)
    )
    far = jnp.abs(sy)
    even = jnp.where(far == kind, 1.0, 0.0)
    odd = jnp.where(far == kind - REACH, jnp.where(sy > 0.0, 1.0, -1.0), 0.0)
    val = jnp.where(kind <= REACH, even, odd)
    kx_q = line + lax.convert_element_type(first, F32)
    val = val * turn(sx * kx_q - jnp.where(lanes < NT, 0.0, 32.0))
    val = jnp.where(kx_q >= lax.convert_element_type(s * L, F32), val, 0.0)
    ones = jnp.where(jnp.logical_and(q == L * NR, lanes < NT), 1.0, 0.0)
    val = jnp.where(q < L * NR, val, ones)
    val_hi = val.astype(BF16)
    at[:, : 2 * NT] = val_hi
    at[:, 2 * NT :] = (val - val_hi.astype(F32)).astype(BF16)
    row = lax.broadcasted_iota(jnp.int32, (2 * REACH, LANE), 0)
    ky = lax.broadcasted_iota(jnp.int32, (2 * REACH, LANE), 1) - 64
    far_row = jnp.where(row < REACH, row + 1, row + 1 - REACH)
    cs[...] = turn((far_row * ky).astype(F32) - jnp.where(row < REACH, 0.0, 32.0))

    def relay(k, carry):
        from_chip = lax.rem(chip + NC - k, NC)
        settle(cbuf.at[:2], ag_rsem.at[from_chip])
        for c in relay_pair(from_chip * 2 + core):
            c.start()
        return carry

    lax.fori_loop(1, NC, relay, 0)
    settle(cbuf.at[:W], mt_rsem)
    settle(xbuf, x_sem)

    onehot = jnp.where(
        gid_ref[...] == lax.broadcasted_iota(jnp.int32, (G, R), 0), 1.0, 0.0
    )
    pick = onehot[:W]
    for l in range(L):
        cols = pl.ds(l * LANE, LANE)
        curves = cbuf[:, 0, cols]
        row = dot(pick, curves, TN_DIMS, HIGH)
        noise = nbuf[:, pl.ds(pl.multiple_of(start + l * LANE, LANE), LANE)]
        x_re = xbuf[0, :, cols].astype(F32)
        x_im = xbuf[1, :, cols].astype(F32)
        gain = noise * row
        re, im = pl.ds(2 * l * LANE, LANE), pl.ds((2 * l + 1) * LANE, LANE)
        wgt[:, re] = (gain * x_re).astype(BF16)
        wgt[:, im] = (gain * x_im).astype(BF16)
        rowbuf[:, cols] = row

    def sc_copy(b, d):
        rows = pl.ds(pl.multiple_of(b * RB, RB), RB)
        return remote(
            sc.at[rows], scr.at[d - 1, rows], sc_ssem, sc_rsem.at[d - 1, b],
            shift=lax.rem(s + d, S),
        )

    def score_block(b, carry):
        acc = jnp.zeros((2 * RB, R), F32)
        for l in range(L):
            cols = pl.ds(l * LANE, LANE)
            ct, st = cos_t[:, cols], sin_t[:, cols]
            rots = []
            for h in range(2):
                for q in range(QB):
                    o = h * H + b * QB + q
                    pair = pbuf[o, :, cols].astype(F32)
                    pr, pi = pair[0:1], pair[1:2]
                    rots.append(
                        jnp.concatenate(
                            [(pr * ct + pi * st).astype(BF16), (pi * ct - pr * st).astype(BF16)],
                            axis=1,
                        )
                    )
            rot = jnp.concatenate(rots, axis=0)
            acc = acc + dot(rot, wgt[:, pl.ds(2 * l * LANE, 2 * LANE)], NT_DIMS)
        both = jnp.concatenate([acc[:RB], acc[RB:]], axis=1)
        sc[pl.ds(pl.multiple_of(b * RB, RB), RB), :] = both
        for d in range(1, S):
            sc_copy(b, d).start()
        return carry

    lax.fori_loop(0, NB, score_block, 0)

    def square(o, carry):
        p = pbuf[o].astype(F32)
        power[pl.ds(o, 1), :] = jnp.sum(p * p, axis=0, keepdims=True)
        return carry

    lax.fori_loop(0, W, square, 0)
    for l in range(L):
        cols = pl.ds(l * LANE, LANE)
        curves = cbuf[:, 0, cols]
        noise = nbuf[:, pl.ds(pl.multiple_of(start + l * LANE, LANE), LANE)]
        here = jnp.where(first + l >= s * L, 0.5, 0.0)
        wsq[:, cols] = curves * curves * noise * here
    self_g = dot(power[...], wsq[...], NT_DIMS, HIGH)
    self_i = dot(self_g, pick, NN_DIMS, HIGH)
    selfc[...] = jnp.concatenate([self_i[:H], self_i[H:]], axis=1)

    def self_copy(d):
        return remote(
            selfc, selfr.at[d - 1], sf_ssem, sc_rsem.at[d - 1, NB],
            shift=lax.rem(s + d, S),
        )

    for d in range(1, S):
        self_copy(d).start()
    for l in range(L):
        cols = pl.ds(l * LANE, LANE)
        row = rowbuf[:, cols]
        f_re = row * xbuf[0, :, cols].astype(F32)
        f_im = row * xbuf[1, :, cols].astype(F32)
        re, im = pl.ds(2 * l * LANE, LANE), pl.ds((2 * l + 1) * LANE, LANE)
        fil[:, re] = jnp.concatenate([f_re, -f_im], axis=0).astype(BF16)
        fil[:, im] = jnp.concatenate([f_im, f_re], axis=0).astype(BF16)
    self_all = selfc[...]
    for d in range(1, S):
        self_copy(d).wait_recv()
        self_all = self_all + selfr[d - 1]
    selft[...] = self_all

    def swap(v):
        return pltpu.roll(v, R, 1)

    def join(b, m):
        rows = pl.ds(pl.multiple_of(b * RB, RB), RB)
        v = sc[rows, :]
        for d in range(1, S):
            sc_copy(b, d).wait_recv()
            v = v + scr[d - 1, rows, :]
        for q in range(QB):
            u = v[q * NT : (q + 1) * NT] - selft[pl.ds(b * QB + q, 1), :]
            tot[pl.ds(pl.multiple_of(b * RB + q * NT, NT), NT), :] = u
            m = jnp.maximum(m, jnp.max(u.reshape(NT // 8, 8, 2 * R), axis=0))
        return m

    m8 = lax.fori_loop(0, NB, join, jnp.full((8, 2 * R), -jnp.inf, F32))
    top = jnp.max(m8, axis=0, keepdims=True)
    top = jnp.maximum(top, swap(top))

    def expo(b, t):
        rows = pl.ds(pl.multiple_of(b * RB, RB), RB)
        e = jnp.exp(tot[rows, :] - top)
        tot[rows, :] = e
        return t + jnp.sum(e.reshape(RB // 8, 8, 2 * R), axis=0)

    t8 = lax.fori_loop(0, NB, expo, jnp.zeros((8, 2 * R), F32))
    total = jnp.sum(t8, axis=0, keepdims=True)
    total = total + swap(total)
    evb[...] = (top + jnp.log(total))[:, :R]
    ev_copy = pltpu.make_async_copy(evb, ev_ref, o_sem.at[0])
    ev_copy.start()

    half = lax.broadcasted_iota(jnp.int32, (NT, 2 * R), 1) < R
    for o in range(H):
        v = tot[o * NT : (o + 1) * NT, :] / total
        a, b = jnp.where(half, v, 0.0), jnp.where(half, 0.0, v)
        cols = []
        for lo, hi in ((a, swap(a)), (swap(b), b)):
            two = jnp.concatenate([lo, hi], axis=0).astype(BF16)
            cols.append(jnp.concatenate([two, two], axis=0))
        out = dot(at[...], jnp.concatenate(cols, axis=1))
        for h in range(2):
            n = h * H + o
            w2[pl.ds((n % 2) * H + n // 2, qn, stride=W), :] = out[:, h * 2 * R : (h + 1) * 2 * R]

    pieces = cuts(L)
    NP = len(pieces)

    def span(c):
        lo, hi = pieces[c]
        return 2 * lo * LANE, 2 * hi * LANE + (G if c == NP - 1 else 0)

    def r1_copy(c):
        lo, hi = span(c)
        rows = pl.ds(pl.multiple_of((1 - core) * H, 8), H)
        return remote(
            part.at[rows, lo:hi], r1.at[:, lo:hi], r1_ssem, r1_rsem.at[c], wide=mate
        )

    RP = stage.shape[0] // NC // NP

    def r2_copy(k, c):
        to = chip_at(k)
        rows = pl.ds(pl.multiple_of(c * RP, 8), RP)
        return remote(
            snd.at[to, rows], r2.at[k, rows], r2_ssem, r2_rsem.at[c],
            wide=2 * to + core,
        )

    mine = pl.ds(pl.multiple_of(core * H, 8), H)
    waves = cs[...]

    def update(c):
        lo, hi = pieces[c]
        for l in range(lo, hi):
            lhs = w2[l * NR * W : (l + 1) * NR * W, :].astype(BF16)
            u = dot(lhs, fil[:, 2 * l * LANE : (2 * l + 2) * LANE])
            u_re, u_im = u[:, :LANE], u[:, LANE:]
            re, im = u_re[:W], u_im[:W]
            for r in range(REACH):
                e = slice((r + 1) * W, (r + 2) * W)
                d = slice((r + 1 + REACH) * W, (r + 2 + REACH) * W)
                c_r, s_r = waves[r : r + 1], waves[REACH + r : REACH + r + 1]
                re = re + (u_re[e] * c_r - u_im[d] * s_r)
                im = im + (u_im[e] * c_r + u_re[d] * s_r)
            part[:, 2 * l * LANE : (2 * l + 1) * LANE] = re
            part[:, (2 * l + 1) * LANE : (2 * l + 2) * LANE] = im
        if c == NP - 1:
            load = w2[L * NR * W : L * NR * W + W, :R]
            part[:, 2 * C : 2 * C + G] = dot(load, onehot, NT_DIMS, HIGH)

    def put(c, i, v):
        stage[pl.ds(c * NC * RP + i, NC, stride=RP), :] = v

    def pass_on(c):
        r1_copy(c).wait_recv()
        lo, hi = pieces[c]
        for i in range(2 * (hi - lo)):
            cols = pl.ds((2 * lo + i) * LANE, LANE)
            put(c, i, part[mine, cols] + r1[:, cols])
        if c == NP - 1:
            for g in range(G // LANE):
                cols = pl.ds(2 * C + g * LANE, LANE)
                rest = part[mine, cols] + r1[:, cols]
                for p in range(3):
                    top_part = rest.astype(BF16).astype(F32)
                    put(c, 2 * (hi - lo) + 3 * g + p, top_part)
                    rest = rest - top_part
        for j in range(NC):
            at_row = (c * NC + j) * RP
            snd[j, c * RP : (c + 1) * RP, :] = stage[at_row : at_row + RP, :].astype(BF16)

        def go(k, carry):
            r2_copy(k, c).start()
            return carry

        lax.fori_loop(1, NC, go, 0)

    for c in range(NP):
        update(c)
        r1_copy(c).start()
        if c:
            pass_on(c - 1)
    pass_on(NP - 1)
    curves = cbuf[:, 0, :]
    squares = curves * curves
    for c in range(NP):
        def take(k, acc):
            return acc + r2[k, c * RP : (c + 1) * RP, :].astype(F32)

        settle(r2.at[1:, c * RP : (c + 1) * RP], r2_rsem.at[c])
        own_rows = stage[pl.ds(pl.multiple_of((c * NC + chip) * RP, 8), RP), :]
        acc = lax.fori_loop(1, NC, take, own_rows)
        lo, hi = pieces[c]
        for l in range(lo, hi):
            i = 2 * (l - lo)
            fbuf[s, l : l + 1, :] = acc[i : i + 1]
            fbuf[s, L + l : L + l + 1, :] = acc[i + 1 : i + 2]
    base = 2 * (pieces[-1][1] - pieces[-1][0])
    load = jnp.concatenate(
        [
            acc[base + 3 * g : base + 3 * g + 1]
            + acc[base + 3 * g + 1 : base + 3 * g + 2]
            + acc[base + 3 * g + 2 : base + 3 * g + 3]
            for g in range(G // LANE)
        ],
        axis=1,
    )[:, :W]
    spread = dot(load, squares, precision=HIGH)
    for l in range(L):
        fbuf[s, 2 * L + l : 2 * L + l + 1, :] = spread[:, l * LANE : (l + 1) * LANE]

    def f_copy(d):
        return remote(
            fbuf.at[s], fbuf.at[s], f_ssem, f_rsem, shift=lax.rem(s + d, S)
        )

    for d in range(1, S):
        f_copy(d).start()
    settle(fbuf.at[: S - 1], f_rsem)
    for t in range(S):
        lo, hi = t * L, min(t * L + L, nl)
        if lo < hi:
            off = lo - min(lo, nl - L)
            for r in range(3):
                obuf[r * nl + lo : r * nl + hi, :] = fbuf[t, r * L + off : r * L + off + hi - lo, :]
    out_copy = pltpu.make_async_copy(obuf, out_ref, o_sem.at[1])
    out_copy.start()

    settle(shbuf.at[: S - 1], sh_ssem)
    settle(cbuf.at[: W - 1], ag_ssem.at[0])
    settle(pbuf.at[: W - 1], ag_ssem.at[1])
    settle(r1, r1_ssem)
    settle(snd.at[: NC - 1], r2_ssem)
    settle(scr.at[: S - 1], sc_ssem)
    settle(selfr.at[: S - 1], sf_ssem)
    settle(fbuf.at[: S - 1], f_ssem)
    ev_copy.wait()
    out_copy.wait()


def unfold(rows_ref, ev_in, out_ref, ev_ref):
    for r in range(rows_ref.shape[0]):
        out_ref[:, r * LANE : (r + 1) * LANE] = rows_ref[r : r + 1, :]
    ev_ref[...] = ev_in[...]


def local(W, S, particles, group_id, ctf_curves, projections, inv_noise, shifts):
    R = particles.shape[0]
    coeffs = inv_noise.shape[0]
    nl = coeffs // LANE
    L = -(-nl // S)
    C = L * LANE
    NTL = shifts.shape[0]
    NT = NTL * S
    H = W // 2
    NB = H // 2
    G = padded(W, LANE)
    rows = H * NT
    qn = padded(L * NR + 1, 16)
    pieces = cuts(L)
    RP = padded(max(2 * (hi - lo) for lo, hi in pieces) + 3 * G // LANE, 16)
    NP = len(pieces)
    any_spec = pl.BlockSpec(memory_space=pl.ANY)
    vm = pl.BlockSpec(memory_space=pltpu.VMEM)
    dma = pltpu.SemaphoreType.DMA
    V = pltpu.VMEM
    out, ev = pl.pallas_call(
        functools.partial(kernel, (W, S, nl, L, NTL, R)),
        out_shape=(
            jax.ShapeDtypeStruct((3 * nl, LANE), F32),
            jax.ShapeDtypeStruct((1, R), F32),
        ),
        in_specs=[any_spec] * 6,
        out_specs=(any_spec, any_spec),
        scratch_shapes=[
            V((1, R), jnp.int32),
            V((2, R, C), BF16),
            V((W, 1, C), F32),
            V((W, 2, C), BF16),
            V((S, 2, NTL), jnp.int32),
            V((1, 2 * coeffs), BF16),
            V((1, coeffs), F32),
            V((NT, C), F32),
            V((NT, C), F32),
            V((R, 2 * C), BF16),
            V((2 * R, 2 * C), BF16),
            V((1, R), F32),
            V((W, C), F32),
            V((W, C), F32),
            V((H, 2 * R), F32),
            V((max(S - 1, 1), H, 2 * R), F32),
            V((H, 2 * R), F32),
            V((R, C), F32),
            V((rows, 2 * R), F32),
            V((max(S - 1, 1), rows, 2 * R), F32),
            V((rows, 2 * R), F32),
            V((qn, 4 * NT), BF16),
            V((2 * REACH, LANE), F32),
            V((qn * W, 2 * R), F32),
            V((W, 2 * C + G), F32),
            V((H, 2 * C + G), F32),
            V((H * NP * RP, LANE), F32),
            V((H, NP * RP, LANE), BF16),
            V((H, NP * RP, LANE), BF16),
            V((S, padded(3 * L, 8), LANE), F32),
            V((3 * nl, LANE), F32),
            dma(()), dma((5,)),
            dma((2,)), dma((W // 2,)), dma(()), dma(()), dma(()),
            dma(()), dma(()), dma((max(S - 1, 1), NB + 1)),
            dma(()), dma((NP,)), dma(()), dma((NP,)),
            dma(()), dma(()), dma((2,)),
        ],
        compiler_params=pltpu.CompilerParams(
            collective_id=0, has_side_effects=True, vmem_limit_bytes=60 * 1024 * 1024
        ),
    )(
        particles, group_id.reshape(1, R), ctf_curves, projections, inv_noise, shifts.T,
    )
    out, ev = pl.pallas_call(
        unfold,
        out_shape=(
            jax.ShapeDtypeStruct((1, 3 * coeffs), F32),
            jax.ShapeDtypeStruct((1, R), F32),
        ),
        in_specs=[vm, vm],
        out_specs=(vm, vm),
    )(out, ev)
    return out, ev.reshape(R)


def solution(mesh):
    W, S = mesh.shape["wide"], mesh.shape["shift"]
    placed = (
        P("wide", None),
        P("wide", None),
        P("wide", None),
        P("wide", None),
        P(),
        P("shift", None),
    )
    return jax.shard_map(
        functools.partial(local, W, S), mesh=mesh, in_specs=placed,
        out_specs=(P("wide", None), P("wide")), check_vma=False,
    )
```

```python
import functools
import math

import jax
import jax.numpy as jnp
from jax import lax
from jax.experimental import pallas as pl
from jax.experimental.pallas import tpu as pltpu
from jax.sharding import PartitionSpec as P

LANE = 128
REACH = 8
FULL = 32767.0
NR = 2 * REACH + 1
PARTS = 3
STEP = 2.0 * math.pi / 128.0
HIGH = lax.Precision.HIGHEST
MESH = pl.DeviceIdType.MESH
F32 = jnp.float32
BF16 = jnp.bfloat16
NT_DIMS = (((1,), (1,)), ((), ()))
NN_DIMS = (((1,), (0,)), ((), ()))
TN_DIMS = (((0,), (0,)), ((), ()))


def dot(a, b, dims=NN_DIMS, precision=None):
    return lax.dot_general(a, b, dims, precision=precision, preferred_element_type=F32)


def turn(m):
    x = m - 128.0 * jnp.floor(m * (1.0 / 128.0) + 0.5)
    z = (32.0 - jnp.abs(x)) * STEP
    y = z * z
    p = 1.0 / 362880.0 - y * (1.0 / 39916800.0)
    p = -1.0 / 5040.0 + y * p
    p = 1.0 / 120.0 + y * p
    p = -1.0 / 6.0 + y * p
    return z + z * (y * p)


def cuts(L):
    n = min(PARTS, L)
    return [(L * c // n, L * (c + 1) // n) for c in range(n)]


def padded(n, m):
    return -(-n // m) * m


def kernel(
    cfg, x_hbm, gid_hbm, ctf_ref, proj_ref, noise_ref, sh_ref,
    out_ref, ev_ref,
    gid_ref, xbuf, cbuf, pbuf, shbuf, prow, nbuf, cos_t, sin_t, wgt, fil, evb, wsq, power, selfc, selfr, selft, rowbuf,
    sc, scr, tot, at, cs, w2, part, r1, stage, snd, r2, fbuf, obuf,
    x_sem, own_sem, ag_ssem, ag_rsem, mt_rsem, sh_ssem, sh_rsem,
    sc_ssem, sf_ssem, sc_rsem, r1_ssem, r1_rsem, r2_ssem, r2_rsem, f_ssem, f_rsem, o_sem,
):
    W, S, nl, L, NTL, R = cfg
    C = L * LANE
    NT = NTL * S
    H = W // 2
    NC = W // 2
    QB = 2
    NB = H // QB
    RB = QB * NT
    w = lax.axis_index("wide")
    s = lax.axis_index("shift")
    core = lax.rem(w, 2)
    chip = lax.div(w, 2)
    mate = chip * 2 + (1 - core)
    first = jnp.minimum(s * L, nl - L)
    start = pl.multiple_of(first * LANE, LANE)
    full = nl * LANE
    G = padded(W, LANE)
    window = pl.ds(start, C)

    def chip_at(k):
        return lax.rem(chip + k, NC)

    def remote(src, dst, ssem, rsem, wide=None, shift=None):
        return pltpu.make_async_remote_copy(
            src_ref=src, dst_ref=dst, send_sem=ssem, recv_sem=rsem,
            device_id=(w if wide is None else wide, s if shift is None else shift),
            device_id_type=MESH,
        )

    def settle(ref, sem):
        pltpu.make_async_copy(ref, ref, sem).wait()

    x_copies = [
        pltpu.make_async_copy(
            x_hbm.at[:, pl.ds(pl.multiple_of(start + h * full, LANE), C)],
            xbuf.at[h], x_sem,
        )
        for h in range(2)
    ]
    own = [
        pltpu.make_async_copy(ctf_ref.at[:, window], cbuf.at[w], own_sem.at[0]),
        pltpu.make_async_copy(proj_ref, prow, own_sem.at[1]),
        pltpu.make_async_copy(sh_ref, shbuf.at[s], own_sem.at[2]),
        pltpu.make_async_copy(noise_ref, nbuf.at[0], own_sem.at[3]),
        pltpu.make_async_copy(gid_hbm, gid_ref, own_sem.at[4]),
    ]
    for c in own + x_copies:
        c.start()

    bar = pltpu.get_barrier_semaphore()
    pl.semaphore_signal(bar, inc=1, device_id=(mate, s), device_id_type=MESH)

    def greet(k, carry):
        pl.semaphore_signal(
            bar, inc=1, device_id=(chip_at(k) * 2 + core, s), device_id_type=MESH
        )
        return carry

    lax.fori_loop(1, NC, greet, 0)
    for d in range(1, S):
        pl.semaphore_signal(
            bar, inc=1, device_id=(w, lax.rem(s + d, S)), device_id_type=MESH
        )
    own[1].wait()
    for h in range(2):
        pbuf[w, h : h + 1, :] = prow[:, pl.ds(pl.multiple_of(start + h * full, LANE), C)]

    pl.semaphore_wait(bar, NC + S - 1)

    def ag_pair(to, rsem):
        return (
            remote(ctf_ref.at[:, window], cbuf.at[w], ag_ssem.at[0], rsem, wide=to),
            remote(pbuf.at[w], pbuf.at[w], ag_ssem.at[1], rsem, wide=to),
        )

    def relay_pair(src):
        return (
            remote(cbuf.at[src], cbuf.at[src], ag_ssem.at[0], mt_rsem, wide=mate),
            remote(pbuf.at[src], pbuf.at[src], ag_ssem.at[1], mt_rsem, wide=mate),
        )

    sh_copies = [
        remote(sh_ref, shbuf.at[s], sh_ssem, sh_rsem, shift=lax.rem(s + d, S))
        for d in range(1, S)
    ]
    for c in sh_copies:
        c.start()

    def ag_start(k, carry):
        for c in ag_pair(chip_at(k) * 2 + core, ag_rsem.at[chip]):
            c.start()
        return carry

    lax.fori_loop(1, NC, ag_start, 0)
    for c in ag_pair(mate, mt_rsem):
        c.start()

    for c in own[:1] + own[2:]:
        c.wait()
    settle(shbuf.at[: S - 1], sh_rsem)

    lane = lax.broadcasted_iota(jnp.int32, (2, 2 * LANE), 1)
    axis = lax.broadcasted_iota(jnp.int32, (2, 2 * LANE), 0)
    freq = jnp.where(
        lane < LANE, jnp.where(axis == 0, first + lane, 0), jnp.where(axis == 1, lane - LANE - 64, 0)
    ).astype(F32)
    ang = STEP * jnp.concatenate(
        [dot(shbuf[t].astype(F32), freq, TN_DIMS, HIGH) for t in range(S)], axis=0
    )
    ang_a, ang_b = ang[:, :LANE], ang[:, LANE:]
    kx = first + lax.broadcasted_iota(jnp.int32, (NT, LANE), 1)
    live = jnp.where(kx >= s * L, 1.0, 0.0)
    cos_b, sin_b = jnp.cos(ang_b), jnp.sin(ang_b)
    cos_a, sin_a = jnp.cos(ang_a) * live, jnp.sin(ang_a) * live
    for l in range(L):
        ca, sa = cos_a[:, l : l + 1], sin_a[:, l : l + 1]
        cols = pl.ds(l * LANE, LANE)
        cos_t[:, cols] = ca * cos_b - sa * sin_b
        sin_t[:, cols] = sa * cos_b + ca * sin_b

    qn = at.shape[0]
    q = lax.broadcasted_iota(jnp.int32, (qn, 2 * NT), 0).astype(F32)
    lanes = lax.broadcasted_iota(jnp.int32, (qn, 2 * NT), 1)
    line = jnp.floor((q + 0.5) * (1.0 / NR))
    kind = q - line * NR
    sx, sy = (
        jnp.concatenate([shbuf[t][a : a + 1, :] for t in range(S)] * 2, axis=1).astype(F32)
        for a in range(2)
    )
    far = jnp.abs(sy)
    even = jnp.where(far == kind, 1.0, 0.0)
    odd = jnp.where(far == kind - REACH, jnp.where(sy > 0.0, 1.0, -1.0), 0.0)
    val = jnp.where(kind <= REACH, even, odd)
    kx_q = line + lax.convert_element_type(first, F32)
    val = val * turn(sx * kx_q - jnp.where(lanes < NT, 0.0, 32.0))
    val = jnp.where(kx_q >= lax.convert_element_type(s * L, F32), val, 0.0)
    ones = jnp.where(jnp.logical_and(q == L * NR, lanes < NT), 1.0, 0.0)
    val = jnp.where(q < L * NR, val, ones)
    val_hi = val.astype(BF16)
    at[:, : 2 * NT] = val_hi
    at[:, 2 * NT :] = (val - val_hi.astype(F32)).astype(BF16)
    row = lax.broadcasted_iota(jnp.int32, (2 * REACH, LANE), 0)
    ky = lax.broadcasted_iota(jnp.int32, (2 * REACH, LANE), 1) - 64
    far_row = jnp.where(row < REACH, row + 1, row + 1 - REACH)
    cs[...] = turn((far_row * ky).astype(F32) - jnp.where(row < REACH, 0.0, 32.0))

    def square(o, carry):
        p = pbuf[o].astype(F32)
        power[pl.ds(o, 1), :] = jnp.sum(p * p, axis=0, keepdims=True)
        return carry

    square(w, 0)

    def relay(k, carry):
        from_chip = lax.rem(chip + NC - k, NC)
        settle(cbuf.at[:2], ag_rsem.at[from_chip])
        for c in relay_pair(from_chip * 2 + core):
            c.start()
        return square(from_chip * 2 + core, carry)

    lax.fori_loop(1, NC, relay, 0)
    settle(cbuf.at[:W], mt_rsem)
    settle(xbuf, x_sem)

    onehot = jnp.where(
        gid_ref[...] == lax.broadcasted_iota(jnp.int32, (G, R), 0), 1.0, 0.0
    )
    pick = onehot[:W]
    for l in range(L):
        cols = pl.ds(l * LANE, LANE)
        curves = cbuf[:, 0, cols]
        row = dot(pick, curves, TN_DIMS, HIGH)
        noise = nbuf[:, pl.ds(pl.multiple_of(start + l * LANE, LANE), LANE)]
        x_re = xbuf[0, :, cols].astype(F32)
        x_im = xbuf[1, :, cols].astype(F32)
        gain = noise * row
        re, im = pl.ds(2 * l * LANE, LANE), pl.ds((2 * l + 1) * LANE, LANE)
        wgt[:, re] = (gain * x_re).astype(BF16)
        wgt[:, im] = (gain * x_im).astype(BF16)
        rowbuf[:, cols] = row

    def sc_copy(b, d):
        rows = pl.ds(pl.multiple_of(b * RB, RB), RB)
        return remote(
            sc.at[rows], scr.at[d - 1, rows], sc_ssem, sc_rsem.at[d - 1, b],
            shift=lax.rem(s + d, S),
        )

    def score_block(b, carry):
        acc = jnp.zeros((2 * RB, R), F32)
        for l in range(L):
            cols = pl.ds(l * LANE, LANE)
            ct, st = cos_t[:, cols], sin_t[:, cols]
            rots = []
            for h in range(2):
                for q in range(QB):
                    o = h * H + b * QB + q
                    pair = pbuf[o, :, cols].astype(F32)
                    pr, pi = pair[0:1], pair[1:2]
                    rots.append(
                        jnp.concatenate(
                            [(pr * ct + pi * st).astype(BF16), (pi * ct - pr * st).astype(BF16)],
                            axis=1,
                        )
                    )
            rot = jnp.concatenate(rots, axis=0)
            acc = acc + dot(rot, wgt[:, pl.ds(2 * l * LANE, 2 * LANE)], NT_DIMS)
        both = jnp.concatenate([acc[:RB], acc[RB:]], axis=1)
        peak = jnp.max(jnp.abs(both).reshape(RB // 8, 8, 2 * R), axis=0)
        peak = jnp.maximum(jnp.max(peak, axis=0, keepdims=True), 1e-30)
        code = jnp.floor(both * (FULL / peak) + 0.5).astype(jnp.int32).astype(jnp.int16)
        sc[pl.ds(pl.multiple_of(b * RB, RB), RB), :] = code
        selfc[pl.ds(H + b, 1), :] = peak * (1.0 / FULL)
        for d in range(1, S):
            sc_copy(b, d).start()
        return carry

    lax.fori_loop(0, NB, score_block, 0)

    def square_mate(j, carry):
        return square(j * 2 + (1 - core), carry)

    lax.fori_loop(0, NC, square_mate, 0)
    for l in range(L):
        cols = pl.ds(l * LANE, LANE)
        curves = cbuf[:, 0, cols]
        noise = nbuf[:, pl.ds(pl.multiple_of(start + l * LANE, LANE), LANE)]
        here = jnp.where(first + l >= s * L, 0.5, 0.0)
        wsq[:, cols] = curves * curves * noise * here
    self_g = dot(power[...], wsq[...], NT_DIMS, HIGH)
    self_i = dot(self_g, pick, NN_DIMS, HIGH)
    selfc[:H, :] = jnp.concatenate([self_i[:H], self_i[H:]], axis=1)

    def self_copy(d):
        return remote(
            selfc, selfr.at[d - 1], sf_ssem, sc_rsem.at[d - 1, NB],
            shift=lax.rem(s + d, S),
        )

    for d in range(1, S):
        self_copy(d).start()
    for l in range(L):
        cols = pl.ds(l * LANE, LANE)
        row = rowbuf[:, cols]
        f_re = row * xbuf[0, :, cols].astype(F32)
        f_im = row * xbuf[1, :, cols].astype(F32)
        re, im = pl.ds(2 * l * LANE, LANE), pl.ds((2 * l + 1) * LANE, LANE)
        fil[:, re] = jnp.concatenate([f_re, -f_im], axis=0).astype(BF16)
        fil[:, im] = jnp.concatenate([f_im, f_re], axis=0).astype(BF16)
    self_all = selfc[:H, :]
    for d in range(1, S):
        self_copy(d).wait_recv()
        self_all = self_all + selfr[d - 1, :H, :]
    selft[...] = self_all

    def swap(v):
        return pltpu.roll(v, R, 1)

    def join(b, m):
        rows = pl.ds(pl.multiple_of(b * RB, RB), RB)
        v = sc[rows, :].astype(jnp.int32).astype(F32) * selfc[pl.ds(H + b, 1), :]
        for d in range(1, S):
            sc_copy(b, d).wait_recv()
            other = scr[d - 1, rows, :].astype(jnp.int32).astype(F32)
            v = v + other * selfr[d - 1, pl.ds(H + b, 1), :]
        for q in range(QB):
            u = v[q * NT : (q + 1) * NT] - selft[pl.ds(b * QB + q, 1), :]
            tot[pl.ds(pl.multiple_of(b * RB + q * NT, NT), NT), :] = u
            m = jnp.maximum(m, jnp.max(u.reshape(NT // 8, 8, 2 * R), axis=0))
        return m

    m8 = lax.fori_loop(0, NB, join, jnp.full((8, 2 * R), -jnp.inf, F32))
    top = jnp.max(m8, axis=0, keepdims=True)
    top = jnp.maximum(top, swap(top))

    def expo(b, t):
        rows = pl.ds(pl.multiple_of(b * RB, RB), RB)
        e = jnp.exp(tot[rows, :] - top)
        tot[rows, :] = e
        return t + jnp.sum(e.reshape(RB // 8, 8, 2 * R), axis=0)

    t8 = lax.fori_loop(0, NB, expo, jnp.zeros((8, 2 * R), F32))
    total = jnp.sum(t8, axis=0, keepdims=True)
    total = total + swap(total)
    evb[...] = (top + jnp.log(total))[:, :R]
    ev_copy = pltpu.make_async_copy(evb, ev_ref, o_sem.at[0])
    ev_copy.start()

    half = lax.broadcasted_iota(jnp.int32, (NT, 2 * R), 1) < R
    for o in range(H):
        v = tot[o * NT : (o + 1) * NT, :] / total
        a, b = jnp.where(half, v, 0.0), jnp.where(half, 0.0, v)
        cols = []
        for lo, hi in ((a, swap(a)), (swap(b), b)):
            two = jnp.concatenate([lo, hi], axis=0).astype(BF16)
            cols.append(jnp.concatenate([two, two], axis=0))
        out = dot(at[...], jnp.concatenate(cols, axis=1))
        for h in range(2):
            n = h * H + o
            w2[pl.ds((n % 2) * H + n // 2, qn, stride=W), :] = out[:, h * 2 * R : (h + 1) * 2 * R]

    pieces = cuts(L)
    NP = len(pieces)

    def span(c):
        lo, hi = pieces[c]
        return 2 * lo * LANE, 2 * hi * LANE + (G if c == NP - 1 else 0)

    def r1_copy(c):
        lo, hi = span(c)
        rows = pl.ds(pl.multiple_of((1 - core) * H, 8), H)
        return remote(
            part.at[rows, lo:hi], r1.at[:, lo:hi], r1_ssem, r1_rsem.at[c], wide=mate
        )

    RP = stage.shape[0] // NC // NP

    def r2_copy(k, c):
        to = chip_at(k)
        rows = pl.ds(pl.multiple_of(c * RP, 8), RP)
        return remote(
            snd.at[to, rows], r2.at[k, rows], r2_ssem, r2_rsem.at[c],
            wide=2 * to + core,
        )

    mine = pl.ds(pl.multiple_of(core * H, 8), H)
    waves = cs[...]

    def update(c):
        lo, hi = pieces[c]
        for l in range(lo, hi):
            lhs = w2[l * NR * W : (l + 1) * NR * W, :].astype(BF16)
            u = dot(lhs, fil[:, 2 * l * LANE : (2 * l + 2) * LANE])
            u_re, u_im = u[:, :LANE], u[:, LANE:]
            re, im = u_re[:W], u_im[:W]
            for r in range(REACH):
                e = slice((r + 1) * W, (r + 2) * W)
                d = slice((r + 1 + REACH) * W, (r + 2 + REACH) * W)
                c_r, s_r = waves[r : r + 1], waves[REACH + r : REACH + r + 1]
                re = re + (u_re[e] * c_r - u_im[d] * s_r)
                im = im + (u_im[e] * c_r + u_re[d] * s_r)
            part[:, 2 * l * LANE : (2 * l + 1) * LANE] = re
            part[:, (2 * l + 1) * LANE : (2 * l + 2) * LANE] = im
        if c == NP - 1:
            load = w2[L * NR * W : L * NR * W + W, :R]
            part[:, 2 * C : 2 * C + G] = dot(load, onehot, NT_DIMS, HIGH)

    def put(c, i, v):
        stage[pl.ds(c * NC * RP + i, NC, stride=RP), :] = v

    def pass_on(c):
        r1_copy(c).wait_recv()
        lo, hi = pieces[c]
        for i in range(2 * (hi - lo)):
            cols = pl.ds((2 * lo + i) * LANE, LANE)
            put(c, i, part[mine, cols] + r1[:, cols])
        if c == NP - 1:
            for g in range(G // LANE):
                cols = pl.ds(2 * C + g * LANE, LANE)
                rest = part[mine, cols] + r1[:, cols]
                for p in range(3):
                    top_part = rest.astype(BF16).astype(F32)
                    put(c, 2 * (hi - lo) + 3 * g + p, top_part)
                    rest = rest - top_part
        for j in range(NC):
            at_row = (c * NC + j) * RP
            snd[j, c * RP : (c + 1) * RP, :] = stage[at_row : at_row + RP, :].astype(BF16)

        def go(k, carry):
            r2_copy(k, c).start()
            return carry

        lax.fori_loop(1, NC, go, 0)

    for c in range(NP):
        update(c)
        r1_copy(c).start()
        if c:
            pass_on(c - 1)
    pass_on(NP - 1)
    curves = cbuf[:, 0, :]
    squares = curves * curves
    for c in range(NP):
        def take(k, acc):
            return acc + r2[k, c * RP : (c + 1) * RP, :].astype(F32)

        settle(r2.at[1:, c * RP : (c + 1) * RP], r2_rsem.at[c])
        own_rows = stage[pl.ds(pl.multiple_of((c * NC + chip) * RP, 8), RP), :]
        acc = lax.fori_loop(1, NC, take, own_rows)
        lo, hi = pieces[c]
        for l in range(lo, hi):
            i = 2 * (l - lo)
            fbuf[s, l : l + 1, :] = acc[i : i + 1]
            fbuf[s, L + l : L + l + 1, :] = acc[i + 1 : i + 2]
    base = 2 * (pieces[-1][1] - pieces[-1][0])
    load = jnp.concatenate(
        [
            acc[base + 3 * g : base + 3 * g + 1]
            + acc[base + 3 * g + 1 : base + 3 * g + 2]
            + acc[base + 3 * g + 2 : base + 3 * g + 3]
            for g in range(G // LANE)
        ],
        axis=1,
    )[:, :W]
    spread = dot(load, squares, precision=HIGH)
    for l in range(L):
        fbuf[s, 2 * L + l : 2 * L + l + 1, :] = spread[:, l * LANE : (l + 1) * LANE]

    def f_copy(d):
        return remote(
            fbuf.at[s], fbuf.at[s], f_ssem, f_rsem, shift=lax.rem(s + d, S)
        )

    for d in range(1, S):
        f_copy(d).start()
    settle(fbuf.at[: S - 1], f_rsem)
    for t in range(S):
        lo, hi = t * L, min(t * L + L, nl)
        if lo < hi:
            off = lo - min(lo, nl - L)
            for r in range(3):
                obuf[r * nl + lo : r * nl + hi, :] = fbuf[t, r * L + off : r * L + off + hi - lo, :]
    out_copy = pltpu.make_async_copy(obuf, out_ref, o_sem.at[1])
    out_copy.start()

    settle(shbuf.at[: S - 1], sh_ssem)
    settle(cbuf.at[: W - 1], ag_ssem.at[0])
    settle(pbuf.at[: W - 1], ag_ssem.at[1])
    settle(r1, r1_ssem)
    settle(snd.at[: NC - 1], r2_ssem)
    settle(scr.at[: S - 1], sc_ssem)
    settle(selfr.at[: S - 1], sf_ssem)
    settle(fbuf.at[: S - 1], f_ssem)
    ev_copy.wait()
    out_copy.wait()


def unfold(rows_ref, ev_in, out_ref, ev_ref):
    for r in range(rows_ref.shape[0]):
        out_ref[:, r * LANE : (r + 1) * LANE] = rows_ref[r : r + 1, :]
    ev_ref[...] = ev_in[...]


def local(W, S, particles, group_id, ctf_curves, projections, inv_noise, shifts):
    R = particles.shape[0]
    coeffs = inv_noise.shape[0]
    nl = coeffs // LANE
    L = -(-nl // S)
    C = L * LANE
    NTL = shifts.shape[0]
    NT = NTL * S
    H = W // 2
    NB = H // 2
    G = padded(W, LANE)
    rows = H * NT
    qn = padded(L * NR + 1, 16)
    pieces = cuts(L)
    RP = padded(max(2 * (hi - lo) for lo, hi in pieces) + 3 * G // LANE, 16)
    NP = len(pieces)
    any_spec = pl.BlockSpec(memory_space=pl.ANY)
    vm = pl.BlockSpec(memory_space=pltpu.VMEM)
    dma = pltpu.SemaphoreType.DMA
    V = pltpu.VMEM
    out, ev = pl.pallas_call(
        functools.partial(kernel, (W, S, nl, L, NTL, R)),
        out_shape=(
            jax.ShapeDtypeStruct((3 * nl, LANE), F32),
            jax.ShapeDtypeStruct((1, R), F32),
        ),
        in_specs=[any_spec] * 6,
        out_specs=(any_spec, any_spec),
        scratch_shapes=[
            V((1, R), jnp.int32),
            V((2, R, C), BF16),
            V((W, 1, C), F32),
            V((W, 2, C), BF16),
            V((S, 2, NTL), jnp.int32),
            V((1, 2 * coeffs), BF16),
            V((1, coeffs), F32),
            V((NT, C), F32),
            V((NT, C), F32),
            V((R, 2 * C), BF16),
            V((2 * R, 2 * C), BF16),
            V((1, R), F32),
            V((W, C), F32),
            V((W, C), F32),
            V((H + NB, 2 * R), F32),
            V((max(S - 1, 1), H + NB, 2 * R), F32),
            V((H, 2 * R), F32),
            V((R, C), F32),
            V((rows, 2 * R), jnp.int16),
            V((max(S - 1, 1), rows, 2 * R), jnp.int16),
            V((rows, 2 * R), F32),
            V((qn, 4 * NT), BF16),
            V((2 * REACH, LANE), F32),
            V((qn * W, 2 * R), F32),
            V((W, 2 * C + G), F32),
            V((H, 2 * C + G), F32),
            V((H * NP * RP, LANE), F32),
            V((H, NP * RP, LANE), BF16),
            V((H, NP * RP, LANE), BF16),
            V((S, padded(3 * L, 8), LANE), F32),
            V((3 * nl, LANE), F32),
            dma(()), dma((5,)),
            dma((2,)), dma((W // 2,)), dma(()), dma(()), dma(()),
            dma(()), dma(()), dma((max(S - 1, 1), NB + 1)),
            dma(()), dma((NP,)), dma(()), dma((NP,)),
            dma(()), dma(()), dma((2,)),
        ],
        compiler_params=pltpu.CompilerParams(
            collective_id=0, has_side_effects=True, vmem_limit_bytes=60 * 1024 * 1024
        ),
    )(
        particles, group_id.reshape(1, R), ctf_curves, projections, inv_noise, shifts.T,
    )
    out, ev = pl.pallas_call(
        unfold,
        out_shape=(
            jax.ShapeDtypeStruct((1, 3 * coeffs), F32),
            jax.ShapeDtypeStruct((1, R), F32),
        ),
        in_specs=[vm, vm],
        out_specs=(vm, vm),
    )(out, ev)
    return out, ev.reshape(R)


def solution(mesh):
    W, S = mesh.shape["wide"], mesh.shape["shift"]
    placed = (
        P("wide", None),
        P("wide", None),
        P("wide", None),
        P("wide", None),
        P(),
        P("shift", None),
    )
    return jax.shard_map(
        functools.partial(local, W, S), mesh=mesh, in_specs=placed,
        out_specs=(P("wide", None), P("wide")), check_vma=False,
    )
```

```python
import functools
import math

import jax
import jax.numpy as jnp
from jax import lax
from jax.experimental import pallas as pl
from jax.experimental.pallas import tpu as pltpu
from jax.sharding import PartitionSpec as P

LANE = 128
REACH = 8
FULL = 32767.0
NR = 2 * REACH + 1
PARTS = 3
STEP = 2.0 * math.pi / 128.0
HIGH = lax.Precision.HIGHEST
MESH = pl.DeviceIdType.MESH
F32 = jnp.float32
BF16 = jnp.bfloat16
NT_DIMS = (((1,), (1,)), ((), ()))
NN_DIMS = (((1,), (0,)), ((), ()))
TN_DIMS = (((0,), (0,)), ((), ()))


def dot(a, b, dims=NN_DIMS, precision=None):
    return lax.dot_general(a, b, dims, precision=precision, preferred_element_type=F32)


def turn(m):
    x = m - 128.0 * jnp.floor(m * (1.0 / 128.0) + 0.5)
    z = (32.0 - jnp.abs(x)) * STEP
    y = z * z
    p = 1.0 / 362880.0 - y * (1.0 / 39916800.0)
    p = -1.0 / 5040.0 + y * p
    p = 1.0 / 120.0 + y * p
    p = -1.0 / 6.0 + y * p
    return z + z * (y * p)


def split3(v):
    hi = v.astype(BF16)
    rest = v - hi.astype(F32)
    mid = rest.astype(BF16)
    return [hi, mid, (rest - mid.astype(F32)).astype(BF16)]


def cuts(L):
    n = min(PARTS, L)
    return [(L * c // n, L * (c + 1) // n) for c in range(n)]


def padded(n, m):
    return -(-n // m) * m


def kernel(
    cfg, x_hbm, gid_hbm, ctf_ref, proj_ref, noise_ref, sh_ref,
    out_ref, ev_ref,
    gid_ref, xbuf, cbuf, pbuf, shbuf, prow, nbuf, cos_t, sin_t, wgt, fil, evb, wsq, power, selfc, selfr, selft, rowbuf,
    sc, scr, tot, at, cs, w2, part, r1, stage, snd, r2, fdat, fwt,
    x_sem, own_sem, ag_ssem, ag_rsem, mt_rsem, sh_ssem, sh_rsem,
    sc_ssem, sf_ssem, sc_rsem, r1_ssem, r1_rsem, r2_ssem, r2_rsem, f_ssem, f_rsem, o_sem,
):
    W, S, nl, L, NTL, R = cfg
    C = L * LANE
    NT = NTL * S
    H = W // 2
    NC = W // 2
    QB = 2
    NB = H // QB
    RB = QB * NT
    w = lax.axis_index("wide")
    s = lax.axis_index("shift")
    core = lax.rem(w, 2)
    chip = lax.div(w, 2)
    mate = chip * 2 + (1 - core)
    first = jnp.minimum(s * L, nl - L)
    start = pl.multiple_of(first * LANE, LANE)
    full = nl * LANE
    G = padded(W, LANE)
    window = pl.ds(start, C)

    def chip_at(k):
        return lax.rem(chip + k, NC)

    def remote(src, dst, ssem, rsem, wide=None, shift=None):
        return pltpu.make_async_remote_copy(
            src_ref=src, dst_ref=dst, send_sem=ssem, recv_sem=rsem,
            device_id=(w if wide is None else wide, s if shift is None else shift),
            device_id_type=MESH,
        )

    def settle(ref, sem):
        pltpu.make_async_copy(ref, ref, sem).wait()

    x_copies = [
        pltpu.make_async_copy(
            x_hbm.at[:, pl.ds(pl.multiple_of(start + h * full, LANE), C)],
            xbuf.at[h], x_sem,
        )
        for h in range(2)
    ]
    own = [
        pltpu.make_async_copy(ctf_ref.at[:, window], cbuf.at[w], own_sem.at[0]),
        pltpu.make_async_copy(proj_ref, prow, own_sem.at[1]),
        pltpu.make_async_copy(sh_ref, shbuf.at[s], own_sem.at[2]),
        pltpu.make_async_copy(noise_ref, nbuf.at[0], own_sem.at[3]),
        pltpu.make_async_copy(gid_hbm, gid_ref, own_sem.at[4]),
    ]
    for c in own + x_copies:
        c.start()

    bar = pltpu.get_barrier_semaphore()
    pl.semaphore_signal(bar, inc=1, device_id=(mate, s), device_id_type=MESH)

    def greet(k, carry):
        pl.semaphore_signal(
            bar, inc=1, device_id=(chip_at(k) * 2 + core, s), device_id_type=MESH
        )
        return carry

    lax.fori_loop(1, NC, greet, 0)
    for d in range(1, S):
        pl.semaphore_signal(
            bar, inc=1, device_id=(w, lax.rem(s + d, S)), device_id_type=MESH
        )
    own[1].wait()
    for h in range(2):
        pbuf[w, h : h + 1, :] = prow[:, pl.ds(pl.multiple_of(start + h * full, LANE), C)]

    pl.semaphore_wait(bar, NC + S - 1)

    def ag_pair(to, rsem):
        return (
            remote(ctf_ref.at[:, window], cbuf.at[w], ag_ssem.at[0], rsem, wide=to),
            remote(pbuf.at[w], pbuf.at[w], ag_ssem.at[1], rsem, wide=to),
        )

    def relay_pair(src):
        return (
            remote(cbuf.at[src], cbuf.at[src], ag_ssem.at[0], mt_rsem, wide=mate),
            remote(pbuf.at[src], pbuf.at[src], ag_ssem.at[1], mt_rsem, wide=mate),
        )

    sh_copies = [
        remote(sh_ref, shbuf.at[s], sh_ssem, sh_rsem, shift=lax.rem(s + d, S))
        for d in range(1, S)
    ]
    for c in sh_copies:
        c.start()

    def ag_start(k, carry):
        for c in ag_pair(chip_at(k) * 2 + core, ag_rsem.at[chip]):
            c.start()
        return carry

    lax.fori_loop(1, NC, ag_start, 0)
    for c in ag_pair(mate, mt_rsem):
        c.start()

    for c in own[:1] + own[2:]:
        c.wait()
    settle(shbuf.at[: S - 1], sh_rsem)

    lane = lax.broadcasted_iota(jnp.int32, (2, 2 * LANE), 1)
    axis = lax.broadcasted_iota(jnp.int32, (2, 2 * LANE), 0)
    freq = jnp.where(
        lane < LANE, jnp.where(axis == 0, first + lane, 0), jnp.where(axis == 1, lane - LANE - 64, 0)
    ).astype(F32)
    ang = STEP * jnp.concatenate(
        [dot(shbuf[t].astype(F32), freq, TN_DIMS, HIGH) for t in range(S)], axis=0
    )
    ang_a, ang_b = ang[:, :LANE], ang[:, LANE:]
    kx = first + lax.broadcasted_iota(jnp.int32, (NT, LANE), 1)
    live = jnp.where(kx >= s * L, 1.0, 0.0)
    cos_b, sin_b = jnp.cos(ang_b), jnp.sin(ang_b)
    cos_a, sin_a = jnp.cos(ang_a) * live, jnp.sin(ang_a) * live
    for l in range(L):
        ca, sa = cos_a[:, l : l + 1], sin_a[:, l : l + 1]
        cols = pl.ds(l * LANE, LANE)
        cos_t[:, cols] = ca * cos_b - sa * sin_b
        sin_t[:, cols] = sa * cos_b + ca * sin_b

    qn = at.shape[0]
    q = lax.broadcasted_iota(jnp.int32, (qn, 2 * NT), 0).astype(F32)
    lanes = lax.broadcasted_iota(jnp.int32, (qn, 2 * NT), 1)
    line = jnp.floor((q + 0.5) * (1.0 / NR))
    kind = q - line * NR
    sx, sy = (
        jnp.concatenate([shbuf[t][a : a + 1, :] for t in range(S)] * 2, axis=1).astype(F32)
        for a in range(2)
    )
    far = jnp.abs(sy)
    even = jnp.where(far == kind, 1.0, 0.0)
    odd = jnp.where(far == kind - REACH, jnp.where(sy > 0.0, 1.0, -1.0), 0.0)
    val = jnp.where(kind <= REACH, even, odd)
    kx_q = line + lax.convert_element_type(first, F32)
    val = val * turn(sx * kx_q - jnp.where(lanes < NT, 0.0, 32.0))
    val = jnp.where(kx_q >= lax.convert_element_type(s * L, F32), val, 0.0)
    ones = jnp.where(jnp.logical_and(q == L * NR, lanes < NT), 1.0, 0.0)
    val = jnp.where(q < L * NR, val, ones)
    val_hi = val.astype(BF16)
    at[:, : 2 * NT] = val_hi
    at[:, 2 * NT :] = (val - val_hi.astype(F32)).astype(BF16)
    row = lax.broadcasted_iota(jnp.int32, (2 * REACH, LANE), 0)
    ky = lax.broadcasted_iota(jnp.int32, (2 * REACH, LANE), 1) - 64
    far_row = jnp.where(row < REACH, row + 1, row + 1 - REACH)
    cs[...] = turn((far_row * ky).astype(F32) - jnp.where(row < REACH, 0.0, 32.0))

    def square(o, carry):
        p = pbuf[o].astype(F32)
        power[pl.ds(o, 1), :] = jnp.sum(p * p, axis=0, keepdims=True)
        return carry

    square(w, 0)

    def relay(k, carry):
        from_chip = lax.rem(chip + NC - k, NC)
        settle(cbuf.at[:2], ag_rsem.at[from_chip])
        for c in relay_pair(from_chip * 2 + core):
            c.start()
        return square(from_chip * 2 + core, carry)

    lax.fori_loop(1, NC, relay, 0)
    settle(cbuf.at[:W], mt_rsem)
    settle(xbuf, x_sem)

    onehot = jnp.where(
        gid_ref[...] == lax.broadcasted_iota(jnp.int32, (G, R), 0), 1.0, 0.0
    )
    pick = onehot[:W]
    pick3 = jnp.concatenate([pick] * 3, axis=0).astype(BF16)
    for l in range(L):
        cols = pl.ds(l * LANE, LANE)
        curves = cbuf[:, 0, cols]
        row = dot(pick3, jnp.concatenate(split3(curves), axis=0), TN_DIMS)
        noise = nbuf[:, pl.ds(pl.multiple_of(start + l * LANE, LANE), LANE)]
        x_re = xbuf[0, :, cols].astype(F32)
        x_im = xbuf[1, :, cols].astype(F32)
        gain = noise * row
        re, im = pl.ds(2 * l * LANE, LANE), pl.ds((2 * l + 1) * LANE, LANE)
        wgt[:, re] = (gain * x_re).astype(BF16)
        wgt[:, im] = (gain * x_im).astype(BF16)
        rowbuf[:, cols] = row

    def sc_copy(b, d):
        rows = pl.ds(pl.multiple_of(b * RB, RB), RB)
        return remote(
            sc.at[rows], scr.at[d - 1, rows], sc_ssem, sc_rsem.at[d - 1, b],
            shift=lax.rem(s + d, S),
        )

    def score_block(b, carry):
        acc = jnp.zeros((2 * RB, R), F32)
        for l in range(L):
            cols = pl.ds(l * LANE, LANE)
            ct, st = cos_t[:, cols], sin_t[:, cols]
            rots = []
            for h in range(2):
                for q in range(QB):
                    o = h * H + b * QB + q
                    pair = pbuf[o, :, cols].astype(F32)
                    pr, pi = pair[0:1], pair[1:2]
                    rots.append(
                        jnp.concatenate(
                            [(pr * ct + pi * st).astype(BF16), (pi * ct - pr * st).astype(BF16)],
                            axis=1,
                        )
                    )
            rot = jnp.concatenate(rots, axis=0)
            acc = acc + dot(rot, wgt[:, pl.ds(2 * l * LANE, 2 * LANE)], NT_DIMS)
        both = jnp.concatenate([acc[:RB], acc[RB:]], axis=1)
        peak = jnp.max(jnp.abs(both).reshape(RB // 8, 8, 2 * R), axis=0)
        peak = jnp.maximum(jnp.max(peak, axis=0, keepdims=True), 1e-30)
        code = jnp.floor(both * (FULL / peak) + 0.5).astype(jnp.int32).astype(jnp.int16)
        sc[pl.ds(pl.multiple_of(b * RB, RB), RB), :] = code
        selfc[pl.ds(H + b, 1), :] = peak * (1.0 / FULL)
        for d in range(1, S):
            sc_copy(b, d).start()
        return carry

    lax.fori_loop(0, NB, score_block, 0)

    def square_mate(j, carry):
        return square(j * 2 + (1 - core), carry)

    lax.fori_loop(0, NC, square_mate, 0)
    for l in range(L):
        cols = pl.ds(l * LANE, LANE)
        curves = cbuf[:, 0, cols]
        noise = nbuf[:, pl.ds(pl.multiple_of(start + l * LANE, LANE), LANE)]
        here = jnp.where(first + l >= s * L, 0.5, 0.0)
        wsq[:, cols] = curves * curves * noise * here
    p3, q3 = split3(power[...]), split3(wsq[...])
    left = jnp.concatenate([p3[0], p3[0], p3[1], p3[1], p3[0], p3[2]], axis=1)
    right = jnp.concatenate([q3[0], q3[1], q3[0], q3[1], q3[2], q3[0]], axis=1)
    self_g = dot(left, right, NT_DIMS)
    self_i = dot(jnp.concatenate(split3(self_g), axis=1), pick3)
    selfc[:H, :] = jnp.concatenate([self_i[:H], self_i[H:]], axis=1)

    def self_copy(d):
        return remote(
            selfc, selfr.at[d - 1], sf_ssem, sc_rsem.at[d - 1, NB],
            shift=lax.rem(s + d, S),
        )

    for d in range(1, S):
        self_copy(d).start()
    for l in range(L):
        cols = pl.ds(l * LANE, LANE)
        row = rowbuf[:, cols]
        f_re = row * xbuf[0, :, cols].astype(F32)
        f_im = row * xbuf[1, :, cols].astype(F32)
        re, im = pl.ds(2 * l * LANE, LANE), pl.ds((2 * l + 1) * LANE, LANE)
        fil[:, re] = jnp.concatenate([f_re, -f_im], axis=0).astype(BF16)
        fil[:, im] = jnp.concatenate([f_im, f_re], axis=0).astype(BF16)
    self_all = selfc[:H, :]
    for d in range(1, S):
        self_copy(d).wait_recv()
        self_all = self_all + selfr[d - 1, :H, :]
    selft[...] = self_all

    def swap(v):
        return pltpu.roll(v, R, 1)

    def join(b, m):
        rows = pl.ds(pl.multiple_of(b * RB, RB), RB)
        v = sc[rows, :].astype(jnp.int32).astype(F32) * selfc[pl.ds(H + b, 1), :]
        for d in range(1, S):
            sc_copy(b, d).wait_recv()
            other = scr[d - 1, rows, :].astype(jnp.int32).astype(F32)
            v = v + other * selfr[d - 1, pl.ds(H + b, 1), :]
        for q in range(QB):
            u = v[q * NT : (q + 1) * NT] - selft[pl.ds(b * QB + q, 1), :]
            tot[pl.ds(pl.multiple_of(b * RB + q * NT, NT), NT), :] = u
            m = jnp.maximum(m, jnp.max(u.reshape(NT // 8, 8, 2 * R), axis=0))
        return m

    m8 = lax.fori_loop(0, NB, join, jnp.full((8, 2 * R), -jnp.inf, F32))
    top = jnp.max(m8, axis=0, keepdims=True)
    top = jnp.maximum(top, swap(top))

    def expo(b, t):
        rows = pl.ds(pl.multiple_of(b * RB, RB), RB)
        e = jnp.exp(tot[rows, :] - top)
        tot[rows, :] = e
        return t + jnp.sum(e.reshape(RB // 8, 8, 2 * R), axis=0)

    t8 = lax.fori_loop(0, NB, expo, jnp.zeros((8, 2 * R), F32))
    total = jnp.sum(t8, axis=0, keepdims=True)
    total = total + swap(total)
    evb[...] = (top + jnp.log(total))[:, :R]
    ev_copy = pltpu.make_async_copy(evb, ev_ref, o_sem.at[0])
    ev_copy.start()

    half = lax.broadcasted_iota(jnp.int32, (NT, 2 * R), 1) < R
    for o in range(H):
        v = tot[o * NT : (o + 1) * NT, :] / total
        a, b = jnp.where(half, v, 0.0), jnp.where(half, 0.0, v)
        cols = []
        for lo, hi in ((a, swap(a)), (swap(b), b)):
            two = jnp.concatenate([lo, hi], axis=0).astype(BF16)
            cols.append(jnp.concatenate([two, two], axis=0))
        out = dot(at[...], jnp.concatenate(cols, axis=1))
        for h in range(2):
            n = h * H + o
            w2[pl.ds((n % 2) * H + n // 2, qn, stride=W), :] = out[:, h * 2 * R : (h + 1) * 2 * R]

    pieces = cuts(L)
    NP = len(pieces)

    def span(c):
        lo, hi = pieces[c]
        return 2 * lo * LANE + (G if c else 0), 2 * hi * LANE + G

    def r1_copy(c):
        lo, hi = span(c)
        rows = pl.ds(pl.multiple_of((1 - core) * H, 8), H)
        return remote(
            part.at[rows, lo:hi], r1.at[:, lo:hi], r1_ssem, r1_rsem.at[c], wide=mate
        )

    RP = stage.shape[0] // NC // NP

    def r2_copy(k, c):
        to = chip_at(k)
        rows = pl.ds(pl.multiple_of(c * RP, 8), RP)
        return remote(
            snd.at[to, rows], r2.at[k, rows], r2_ssem, r2_rsem.at[c],
            wide=2 * to + core,
        )

    mine = pl.ds(pl.multiple_of(core * H, 8), H)
    waves = cs[...]

    def update(c):
        lo, hi = pieces[c]
        if c == 0:
            load = w2[L * NR * W : L * NR * W + W, :R]
            part[:, :G] = dot(load, onehot, NT_DIMS, HIGH)
        for l in range(lo, hi):
            lhs = w2[l * NR * W : (l + 1) * NR * W, :].astype(BF16)
            u = dot(lhs, fil[:, 2 * l * LANE : (2 * l + 2) * LANE])
            u_re, u_im = u[:, :LANE], u[:, LANE:]
            re, im = u_re[:W], u_im[:W]
            for r in range(REACH):
                e = slice((r + 1) * W, (r + 2) * W)
                d = slice((r + 1 + REACH) * W, (r + 2 + REACH) * W)
                c_r, s_r = waves[r : r + 1], waves[REACH + r : REACH + r + 1]
                re = re + (u_re[e] * c_r - u_im[d] * s_r)
                im = im + (u_im[e] * c_r + u_re[d] * s_r)
            col = G + 2 * l * LANE
            part[:, col : col + LANE] = re
            part[:, col + LANE : col + 2 * LANE] = im
    def put(c, i, v):
        stage[pl.ds(c * NC * RP + i, NC, stride=RP), :] = v

    def pass_on(c):
        r1_copy(c).wait_recv()
        lo, hi = pieces[c]
        for i in range(2 * (hi - lo)):
            cols = pl.ds(G + (2 * lo + i) * LANE, LANE)
            put(c, i, part[mine, cols] + r1[:, cols])
        if c == 0:
            for g in range(G // LANE):
                cols = pl.ds(g * LANE, LANE)
                rest = part[mine, cols] + r1[:, cols]
                for p in range(3):
                    top_part = rest.astype(BF16).astype(F32)
                    put(c, 2 * (hi - lo) + 3 * g + p, top_part)
                    rest = rest - top_part
        for j in range(NC):
            at_row = (c * NC + j) * RP
            snd[j, c * RP : (c + 1) * RP, :] = stage[at_row : at_row + RP, :].astype(BF16)

        def go(k, carry):
            r2_copy(k, c).start()
            return carry

        lax.fori_loop(1, NC, go, 0)

    for c in range(NP):
        update(c)
        r1_copy(c).start()
        if c:
            pass_on(c - 1)
    pass_on(NP - 1)
    curves = cbuf[:, 0, :]
    squares = curves * curves

    def deliver(src, row):
        dst = out_ref.at[s, row : row + src.shape[0]]
        for d in range(1, S):
            remote(src, dst, f_ssem, f_rsem, shift=lax.rem(s + d, S)).start()
        pltpu.make_async_copy(src, dst, o_sem.at[1]).start()

    for c in range(NP):
        def take(k, acc):
            return acc + r2[k, c * RP : (c + 1) * RP, :].astype(F32)

        settle(r2.at[1:, c * RP : (c + 1) * RP], r2_rsem.at[c])
        own_rows = stage[pl.ds(pl.multiple_of((c * NC + chip) * RP, 8), RP), :]
        acc = lax.fori_loop(1, NC, take, own_rows)
        fdat[c] = acc
        deliver(fdat.at[c], c * RP)
        if c == 0:
            lo, hi = pieces[c]
            base = 2 * (hi - lo)
            load = jnp.concatenate(
                [
                    acc[base + 3 * g : base + 3 * g + 1]
                    + acc[base + 3 * g + 1 : base + 3 * g + 2]
                    + acc[base + 3 * g + 2 : base + 3 * g + 3]
                    for g in range(G // LANE)
                ],
                axis=1,
            )[:, :W]
            spread = dot(load, squares, precision=HIGH)
            for l in range(L):
                fwt[l : l + 1, :] = spread[:, l * LANE : (l + 1) * LANE]
            deliver(fwt, NP * RP)

    settle(out_ref.at[: S - 1], f_rsem)
    settle(shbuf.at[: S - 1], sh_ssem)
    settle(cbuf.at[: W - 1], ag_ssem.at[0])
    settle(pbuf.at[: W - 1], ag_ssem.at[1])
    settle(r1, r1_ssem)
    settle(snd.at[: NC - 1], r2_ssem)
    settle(scr.at[: S - 1], sc_ssem)
    settle(selfr.at[: S - 1], sf_ssem)
    settle(out_ref.at[: S - 1], f_ssem)
    ev_copy.wait()
    settle(out_ref.at[:1], o_sem.at[1])


def unfold(nl, L, RP, rows_ref, ev_in, out_ref, ev_ref):
    S = rows_ref.shape[0]
    pieces = cuts(L)
    for t in range(S):
        first = min(t * L, nl - L)
        for c, (lo, hi) in enumerate(pieces):
            for l in range(lo, hi):
                n = first + l
                if n < t * L:
                    continue
                at_row = c * RP + 2 * (l - lo)
                for r, row in enumerate((at_row, at_row + 1, len(pieces) * RP + l)):
                    col = (r * nl + n) * LANE
                    out_ref[:, col : col + LANE] = rows_ref[t, row : row + 1, :]
    ev_ref[...] = ev_in[...]


def local(W, S, particles, group_id, ctf_curves, projections, inv_noise, shifts):
    R = particles.shape[0]
    coeffs = inv_noise.shape[0]
    nl = coeffs // LANE
    L = -(-nl // S)
    C = L * LANE
    NTL = shifts.shape[0]
    NT = NTL * S
    H = W // 2
    NB = H // 2
    G = padded(W, LANE)
    rows = H * NT
    qn = padded(L * NR + 1, 16)
    pieces = cuts(L)
    RP = padded(max(2 * (hi - lo) for lo, hi in pieces) + 3 * G // LANE, 16)
    NP = len(pieces)
    any_spec = pl.BlockSpec(memory_space=pl.ANY)
    vm = pl.BlockSpec(memory_space=pltpu.VMEM)
    dma = pltpu.SemaphoreType.DMA
    V = pltpu.VMEM
    out, ev = pl.pallas_call(
        functools.partial(kernel, (W, S, nl, L, NTL, R)),
        out_shape=(
            jax.ShapeDtypeStruct((S, NP * RP + padded(L, 8), LANE), F32),
            jax.ShapeDtypeStruct((1, R), F32),
        ),
        in_specs=[any_spec] * 6,
        out_specs=(any_spec, any_spec),
        scratch_shapes=[
            V((1, R), jnp.int32),
            V((2, R, C), BF16),
            V((W, 1, C), F32),
            V((W, 2, C), BF16),
            V((S, 2, NTL), jnp.int32),
            V((1, 2 * coeffs), BF16),
            V((1, coeffs), F32),
            V((NT, C), F32),
            V((NT, C), F32),
            V((R, 2 * C), BF16),
            V((2 * R, 2 * C), BF16),
            V((1, R), F32),
            V((W, C), F32),
            V((W, C), F32),
            V((H + NB, 2 * R), F32),
            V((max(S - 1, 1), H + NB, 2 * R), F32),
            V((H, 2 * R), F32),
            V((R, C), F32),
            V((rows, 2 * R), jnp.int16),
            V((max(S - 1, 1), rows, 2 * R), jnp.int16),
            V((rows, 2 * R), F32),
            V((qn, 4 * NT), BF16),
            V((2 * REACH, LANE), F32),
            V((qn * W, 2 * R), F32),
            V((W, 2 * C + G), F32),
            V((H, 2 * C + G), F32),
            V((H * NP * RP, LANE), F32),
            V((H, NP * RP, LANE), BF16),
            V((H, NP * RP, LANE), BF16),
            V((NP, RP, LANE), F32),
            V((padded(L, 8), LANE), F32),
            dma(()), dma((5,)),
            dma((2,)), dma((W // 2,)), dma(()), dma(()), dma(()),
            dma(()), dma(()), dma((max(S - 1, 1), NB + 1)),
            dma(()), dma((NP,)), dma(()), dma((NP,)),
            dma(()), dma(()), dma((2,)),
        ],
        compiler_params=pltpu.CompilerParams(
            collective_id=0, has_side_effects=True, vmem_limit_bytes=60 * 1024 * 1024
        ),
    )(
        particles, group_id.reshape(1, R), ctf_curves, projections, inv_noise, shifts.T,
    )
    out, ev = pl.pallas_call(
        functools.partial(unfold, nl, L, RP),
        out_shape=(
            jax.ShapeDtypeStruct((1, 3 * coeffs), F32),
            jax.ShapeDtypeStruct((1, R), F32),
        ),
        in_specs=[vm, vm],
        out_specs=(vm, vm),
    )(out, ev)
    return out, ev.reshape(R)


def solution(mesh):
    W, S = mesh.shape["wide"], mesh.shape["shift"]
    placed = (
        P("wide", None),
        P("wide", None),
        P("wide", None),
        P("wide", None),
        P(),
        P("shift", None),
    )
    return jax.shard_map(
        functools.partial(local, W, S), mesh=mesh, in_specs=placed,
        out_specs=(P("wide", None), P("wide")), check_vma=False,
    )
```

```python
import functools
import math

import jax
import jax.numpy as jnp
from jax import lax
from jax.experimental import pallas as pl
from jax.experimental.pallas import tpu as pltpu
from jax.sharding import PartitionSpec as P

LANE = 128
REACH = 8
FULL = 32767.0
NR = 2 * REACH + 1
PARTS = 3
STEP = 2.0 * math.pi / 128.0
HIGH = lax.Precision.HIGHEST
MESH = pl.DeviceIdType.MESH
F32 = jnp.float32
BF16 = jnp.bfloat16
NT_DIMS = (((1,), (1,)), ((), ()))
NN_DIMS = (((1,), (0,)), ((), ()))
TN_DIMS = (((0,), (0,)), ((), ()))


def dot(a, b, dims=NN_DIMS, precision=None):
    return lax.dot_general(a, b, dims, precision=precision, preferred_element_type=F32)


def turn(m):
    x = m - 128.0 * jnp.floor(m * (1.0 / 128.0) + 0.5)
    z = (32.0 - jnp.abs(x)) * STEP
    y = z * z
    p = 1.0 / 362880.0 - y * (1.0 / 39916800.0)
    p = -1.0 / 5040.0 + y * p
    p = 1.0 / 120.0 + y * p
    p = -1.0 / 6.0 + y * p
    return z + z * (y * p)


def split3(v):
    hi = v.astype(BF16)
    rest = v - hi.astype(F32)
    mid = rest.astype(BF16)
    return [hi, mid, (rest - mid.astype(F32)).astype(BF16)]


def cuts(L):
    n = min(PARTS, L)
    return [(L * c // n, L * (c + 1) // n) for c in range(n)]


def padded(n, m):
    return -(-n // m) * m


def kernel(
    cfg, x_hbm, gid_hbm, ctf_ref, proj_ref, noise_ref, sh_ref,
    out_ref, ev_ref,
    gid_ref, xbuf, cbuf, pbuf, shbuf, prow, nbuf, cos_t, sin_t, wgt, fil, evb, wsq, power, selfc, selfr, selft, rowbuf,
    sc, scr, tot, at, cs, w2, part, r1, stage, snd, r2, fdat, fwt,
    x_sem, own_sem, ag_ssem, ag_rsem, mt_rsem, sh_ssem, sh_rsem,
    sc_ssem, sf_ssem, sc_rsem, r1_ssem, r1_rsem, r2_ssem, r2_rsem, f_ssem, f_rsem, o_sem,
):
    W, S, nl, L, NTL, R = cfg
    C = L * LANE
    NT = NTL * S
    H = W // 2
    NC = W // 2
    QB = 2
    NB = H // QB
    RB = QB * NT
    w = lax.axis_index("wide")
    s = lax.axis_index("shift")
    core = lax.rem(w, 2)
    chip = lax.div(w, 2)
    mate = chip * 2 + (1 - core)
    first = jnp.minimum(s * L, nl - L)
    start = pl.multiple_of(first * LANE, LANE)
    full = nl * LANE
    G = padded(W, LANE)
    window = pl.ds(start, C)

    def chip_at(k):
        if NC & (NC - 1):
            return lax.rem(chip + k, NC)
        other, bit = 0, 1
        while bit < NC:
            mine_bit = lax.rem(lax.div(chip, bit), 2)
            other = other + bit * lax.rem(mine_bit + lax.rem(lax.div(k, bit), 2), 2)
            bit *= 2
        return other

    def chip_from(k):
        return lax.rem(chip + NC - k, NC) if NC & (NC - 1) else chip_at(k)

    def remote(src, dst, ssem, rsem, wide=None, shift=None):
        return pltpu.make_async_remote_copy(
            src_ref=src, dst_ref=dst, send_sem=ssem, recv_sem=rsem,
            device_id=(w if wide is None else wide, s if shift is None else shift),
            device_id_type=MESH,
        )

    def settle(ref, sem):
        pltpu.make_async_copy(ref, ref, sem).wait()

    x_copies = [
        pltpu.make_async_copy(
            x_hbm.at[:, pl.ds(pl.multiple_of(start + h * full, LANE), C)],
            xbuf.at[h], x_sem,
        )
        for h in range(2)
    ]
    own = [
        pltpu.make_async_copy(ctf_ref.at[:, window], cbuf.at[w], own_sem.at[0]),
        pltpu.make_async_copy(proj_ref, prow, own_sem.at[1]),
        pltpu.make_async_copy(sh_ref, shbuf.at[s], own_sem.at[2]),
        pltpu.make_async_copy(noise_ref, nbuf.at[0], own_sem.at[3]),
        pltpu.make_async_copy(gid_hbm, gid_ref, own_sem.at[4]),
    ]
    for c in own + x_copies:
        c.start()

    bar = pltpu.get_barrier_semaphore()
    pl.semaphore_signal(bar, inc=1, device_id=(mate, s), device_id_type=MESH)

    def greet(k, carry):
        pl.semaphore_signal(
            bar, inc=1, device_id=(chip_at(k) * 2 + core, s), device_id_type=MESH
        )
        return carry

    lax.fori_loop(1, NC, greet, 0)
    for d in range(1, S):
        pl.semaphore_signal(
            bar, inc=1, device_id=(w, lax.rem(s + d, S)), device_id_type=MESH
        )
    own[1].wait()
    for h in range(2):
        pbuf[w, h : h + 1, :] = prow[:, pl.ds(pl.multiple_of(start + h * full, LANE), C)]

    pl.semaphore_wait(bar, NC + S - 1)

    def ag_pair(to, rsem):
        return (
            remote(ctf_ref.at[:, window], cbuf.at[w], ag_ssem.at[0], rsem, wide=to),
            remote(pbuf.at[w], pbuf.at[w], ag_ssem.at[1], rsem, wide=to),
        )

    def relay_pair(src):
        return (
            remote(cbuf.at[src], cbuf.at[src], ag_ssem.at[0], mt_rsem, wide=mate),
            remote(pbuf.at[src], pbuf.at[src], ag_ssem.at[1], mt_rsem, wide=mate),
        )

    sh_copies = [
        remote(sh_ref, shbuf.at[s], sh_ssem, sh_rsem, shift=lax.rem(s + d, S))
        for d in range(1, S)
    ]
    for c in sh_copies:
        c.start()

    def ag_start(k, carry):
        for c in ag_pair(chip_at(NC - k) * 2 + core, ag_rsem.at[chip]):
            c.start()
        return carry

    lax.fori_loop(1, NC, ag_start, 0)
    for c in ag_pair(mate, mt_rsem):
        c.start()

    for c in own[:1] + own[2:]:
        c.wait()
    settle(shbuf.at[: S - 1], sh_rsem)

    lane = lax.broadcasted_iota(jnp.int32, (2, 2 * LANE), 1)
    axis = lax.broadcasted_iota(jnp.int32, (2, 2 * LANE), 0)
    freq = jnp.where(
        lane < LANE, jnp.where(axis == 0, first + lane, 0), jnp.where(axis == 1, lane - LANE - 64, 0)
    ).astype(F32)
    ang = STEP * jnp.concatenate(
        [dot(shbuf[t].astype(F32), freq, TN_DIMS, HIGH) for t in range(S)], axis=0
    )
    ang_a, ang_b = ang[:, :LANE], ang[:, LANE:]
    kx = first + lax.broadcasted_iota(jnp.int32, (NT, LANE), 1)
    live = jnp.where(kx >= s * L, 1.0, 0.0)
    cos_b, sin_b = jnp.cos(ang_b), jnp.sin(ang_b)
    cos_a, sin_a = jnp.cos(ang_a) * live, jnp.sin(ang_a) * live
    for l in range(L):
        ca, sa = cos_a[:, l : l + 1], sin_a[:, l : l + 1]
        cols = pl.ds(l * LANE, LANE)
        cos_t[:, cols] = ca * cos_b - sa * sin_b
        sin_t[:, cols] = sa * cos_b + ca * sin_b

    qn = at.shape[0]
    q = lax.broadcasted_iota(jnp.int32, (qn, 2 * NT), 0).astype(F32)
    lanes = lax.broadcasted_iota(jnp.int32, (qn, 2 * NT), 1)
    line = jnp.floor((q + 0.5) * (1.0 / NR))
    kind = q - line * NR
    sx, sy = (
        jnp.concatenate([shbuf[t][a : a + 1, :] for t in range(S)] * 2, axis=1).astype(F32)
        for a in range(2)
    )
    far = jnp.abs(sy)
    even = jnp.where(far == kind, 1.0, 0.0)
    odd = jnp.where(far == kind - REACH, jnp.where(sy > 0.0, 1.0, -1.0), 0.0)
    val = jnp.where(kind <= REACH, even, odd)
    kx_q = line + lax.convert_element_type(first, F32)
    val = val * turn(sx * kx_q - jnp.where(lanes < NT, 0.0, 32.0))
    val = jnp.where(kx_q >= lax.convert_element_type(s * L, F32), val, 0.0)
    ones = jnp.where(jnp.logical_and(q == L * NR, lanes < NT), 1.0, 0.0)
    val = jnp.where(q < L * NR, val, ones)
    val_hi = val.astype(BF16)
    at[:, : 2 * NT] = val_hi
    at[:, 2 * NT :] = (val - val_hi.astype(F32)).astype(BF16)
    row = lax.broadcasted_iota(jnp.int32, (2 * REACH, LANE), 0)
    ky = lax.broadcasted_iota(jnp.int32, (2 * REACH, LANE), 1) - 64
    far_row = jnp.where(row < REACH, row + 1, row + 1 - REACH)
    cs[...] = turn((far_row * ky).astype(F32) - jnp.where(row < REACH, 0.0, 32.0))

    def square(o, carry):
        p = pbuf[o].astype(F32)
        power[pl.ds(o, 1), :] = jnp.sum(p * p, axis=0, keepdims=True)
        return carry

    square(w, 0)

    def relay(k, carry):
        from_chip = chip_from(k)
        settle(cbuf.at[:2], ag_rsem.at[from_chip])
        for c in relay_pair(from_chip * 2 + core):
            c.start()
        return square(from_chip * 2 + core, carry)

    lax.fori_loop(1, NC, relay, 0)
    settle(cbuf.at[:W], mt_rsem)
    settle(xbuf, x_sem)

    onehot = jnp.where(
        gid_ref[...] == lax.broadcasted_iota(jnp.int32, (G, R), 0), 1.0, 0.0
    )
    pick = onehot[:W]
    pick3 = jnp.concatenate([pick] * 3, axis=0).astype(BF16)
    for l in range(L):
        cols = pl.ds(l * LANE, LANE)
        curves = cbuf[:, 0, cols]
        row = dot(pick3, jnp.concatenate(split3(curves), axis=0), TN_DIMS)
        noise = nbuf[:, pl.ds(pl.multiple_of(start + l * LANE, LANE), LANE)]
        x_re = xbuf[0, :, cols].astype(F32)
        x_im = xbuf[1, :, cols].astype(F32)
        gain = noise * row
        re, im = pl.ds(2 * l * LANE, LANE), pl.ds((2 * l + 1) * LANE, LANE)
        wgt[:, re] = (gain * x_re).astype(BF16)
        wgt[:, im] = (gain * x_im).astype(BF16)
        rowbuf[:, cols] = row

    def sc_copy(b, d):
        rows = pl.ds(pl.multiple_of(b * RB, RB), RB)
        return remote(
            sc.at[rows], scr.at[d - 1, rows], sc_ssem, sc_rsem.at[d - 1, b],
            shift=lax.rem(s + d, S),
        )

    def score_block(b, carry):
        acc = jnp.zeros((2 * RB, R), F32)
        for l in range(L):
            cols = pl.ds(l * LANE, LANE)
            ct, st = cos_t[:, cols], sin_t[:, cols]
            rots = []
            for h in range(2):
                for q in range(QB):
                    o = h * H + b * QB + q
                    pair = pbuf[o, :, cols].astype(F32)
                    pr, pi = pair[0:1], pair[1:2]
                    rots.append(
                        jnp.concatenate(
                            [(pr * ct + pi * st).astype(BF16), (pi * ct - pr * st).astype(BF16)],
                            axis=1,
                        )
                    )
            rot = jnp.concatenate(rots, axis=0)
            acc = acc + dot(rot, wgt[:, pl.ds(2 * l * LANE, 2 * LANE)], NT_DIMS)
        both = jnp.concatenate([acc[:RB], acc[RB:]], axis=1)
        peak = jnp.max(jnp.abs(both).reshape(RB // 8, 8, 2 * R), axis=0)
        peak = jnp.maximum(jnp.max(peak, axis=0, keepdims=True), 1e-30)
        code = jnp.floor(both * (FULL / peak) + 0.5).astype(jnp.int32).astype(jnp.int16)
        sc[pl.ds(pl.multiple_of(b * RB, RB), RB), :] = code
        selfc[pl.ds(H + b, 1), :] = peak * (1.0 / FULL)
        for d in range(1, S):
            sc_copy(b, d).start()
        return carry

    lax.fori_loop(0, NB, score_block, 0)

    def square_mate(j, carry):
        return square(j * 2 + (1 - core), carry)

    lax.fori_loop(0, NC, square_mate, 0)
    for l in range(L):
        cols = pl.ds(l * LANE, LANE)
        curves = cbuf[:, 0, cols]
        noise = nbuf[:, pl.ds(pl.multiple_of(start + l * LANE, LANE), LANE)]
        here = jnp.where(first + l >= s * L, 0.5, 0.0)
        wsq[:, cols] = curves * curves * noise * here
    p3, q3 = split3(power[...]), split3(wsq[...])
    left = jnp.concatenate([p3[0], p3[0], p3[1]], axis=1)
    right = jnp.concatenate([q3[0], q3[1], q3[0]], axis=1)
    self_g = dot(left, right, NT_DIMS)
    self_i = dot(jnp.concatenate(split3(self_g), axis=1), pick3)
    selfc[:H, :] = jnp.concatenate([self_i[:H], self_i[H:]], axis=1)

    def self_copy(d):
        return remote(
            selfc, selfr.at[d - 1], sf_ssem, sc_rsem.at[d - 1, NB],
            shift=lax.rem(s + d, S),
        )

    for d in range(1, S):
        self_copy(d).start()
    for l in range(L):
        cols = pl.ds(l * LANE, LANE)
        row = rowbuf[:, cols]
        f_re = row * xbuf[0, :, cols].astype(F32)
        f_im = row * xbuf[1, :, cols].astype(F32)
        re, im = pl.ds(2 * l * LANE, LANE), pl.ds((2 * l + 1) * LANE, LANE)
        fil[:, re] = jnp.concatenate([f_re, -f_im], axis=0).astype(BF16)
        fil[:, im] = jnp.concatenate([f_im, f_re], axis=0).astype(BF16)
    self_all = selfc[:H, :]
    for d in range(1, S):
        self_copy(d).wait_recv()
        self_all = self_all + selfr[d - 1, :H, :]
    selft[...] = self_all

    def swap(v):
        return pltpu.roll(v, R, 1)

    def join(b, m):
        rows = pl.ds(pl.multiple_of(b * RB, RB), RB)
        v = sc[rows, :].astype(jnp.int32).astype(F32) * selfc[pl.ds(H + b, 1), :]
        for d in range(1, S):
            sc_copy(b, d).wait_recv()
            other = scr[d - 1, rows, :].astype(jnp.int32).astype(F32)
            v = v + other * selfr[d - 1, pl.ds(H + b, 1), :]
        for q in range(QB):
            u = v[q * NT : (q + 1) * NT] - selft[pl.ds(b * QB + q, 1), :]
            tot[pl.ds(pl.multiple_of(b * RB + q * NT, NT), NT), :] = u
            m = jnp.maximum(m, jnp.max(u.reshape(NT // 8, 8, 2 * R), axis=0))
        return m

    m8 = lax.fori_loop(0, NB, join, jnp.full((8, 2 * R), -jnp.inf, F32))
    top = jnp.max(m8, axis=0, keepdims=True)
    top = jnp.maximum(top, swap(top))

    def expo(b, t):
        rows = pl.ds(pl.multiple_of(b * RB, RB), RB)
        e = jnp.exp(tot[rows, :] - top)
        tot[rows, :] = e
        return t + jnp.sum(e.reshape(RB // 8, 8, 2 * R), axis=0)

    t8 = lax.fori_loop(0, NB, expo, jnp.zeros((8, 2 * R), F32))
    total = jnp.sum(t8, axis=0, keepdims=True)
    total = total + swap(total)
    evb[...] = (top + jnp.log(total))[:, :R]
    ev_copy = pltpu.make_async_copy(evb, ev_ref, o_sem.at[0])
    ev_copy.start()

    half = lax.broadcasted_iota(jnp.int32, (NT, 2 * R), 1) < R
    for o in range(H):
        v = tot[o * NT : (o + 1) * NT, :] / total
        a, b = jnp.where(half, v, 0.0), jnp.where(half, 0.0, v)
        cols = []
        for lo, hi in ((a, swap(a)), (swap(b), b)):
            two = jnp.concatenate([lo, hi], axis=0).astype(BF16)
            cols.append(jnp.concatenate([two, two], axis=0))
        out = dot(at[...], jnp.concatenate(cols, axis=1))
        for h in range(2):
            n = h * H + o
            w2[pl.ds((n % 2) * H + n // 2, qn, stride=W), :] = out[:, h * 2 * R : (h + 1) * 2 * R]

    pieces = cuts(L)
    NP = len(pieces)

    def span(c):
        lo, hi = pieces[c]
        return 2 * lo * LANE + (G if c else 0), 2 * hi * LANE + G

    def r1_copy(c):
        lo, hi = span(c)
        rows = pl.ds(pl.multiple_of((1 - core) * H, 8), H)
        return remote(
            part.at[rows, lo:hi], r1.at[:, lo:hi], r1_ssem, r1_rsem.at[c], wide=mate
        )

    RP = stage.shape[0] // NC // NP

    def r2_copy(k, c):
        to = chip_at(k)
        rows = pl.ds(pl.multiple_of(c * RP, 8), RP)
        return remote(
            snd.at[to, rows], r2.at[k, rows], r2_ssem, r2_rsem.at[c],
            wide=2 * to + core,
        )

    mine = pl.ds(pl.multiple_of(core * H, 8), H)
    waves = cs[...]

    def update(c):
        lo, hi = pieces[c]
        if c == 0:
            load = w2[L * NR * W : L * NR * W + W, :R]
            part[:, :G] = dot(load, onehot, NT_DIMS, HIGH)
        for l in range(lo, hi):
            lhs = w2[l * NR * W : (l + 1) * NR * W, :].astype(BF16)
            u = dot(lhs, fil[:, 2 * l * LANE : (2 * l + 2) * LANE])
            u_re, u_im = u[:, :LANE], u[:, LANE:]
            re, im = u_re[:W], u_im[:W]
            for r in range(REACH):
                e = slice((r + 1) * W, (r + 2) * W)
                d = slice((r + 1 + REACH) * W, (r + 2 + REACH) * W)
                c_r, s_r = waves[r : r + 1], waves[REACH + r : REACH + r + 1]
                re = re + (u_re[e] * c_r - u_im[d] * s_r)
                im = im + (u_im[e] * c_r + u_re[d] * s_r)
            col = G + 2 * l * LANE
            part[:, col : col + LANE] = re
            part[:, col + LANE : col + 2 * LANE] = im
    def put(c, i, v):
        stage[pl.ds(c * NC * RP + i, NC, stride=RP), :] = v

    def pass_on(c):
        r1_copy(c).wait_recv()
        lo, hi = pieces[c]
        for i in range(2 * (hi - lo)):
            cols = pl.ds(G + (2 * lo + i) * LANE, LANE)
            put(c, i, part[mine, cols] + r1[:, cols])
        if c == 0:
            for g in range(G // LANE):
                cols = pl.ds(g * LANE, LANE)
                rest = part[mine, cols] + r1[:, cols]
                for p in range(3):
                    top_part = rest.astype(BF16).astype(F32)
                    put(c, 2 * (hi - lo) + 3 * g + p, top_part)
                    rest = rest - top_part
        for j in range(NC):
            at_row = (c * NC + j) * RP
            snd[j, c * RP : (c + 1) * RP, :] = stage[at_row : at_row + RP, :].astype(BF16)

        def go(k, carry):
            r2_copy(NC - k, c).start()
            return carry

        lax.fori_loop(1, NC, go, 0)

    for c in range(NP):
        update(c)
        r1_copy(c).start()
        if c:
            pass_on(c - 1)
    pass_on(NP - 1)
    curves = cbuf[:, 0, :]
    squares = curves * curves

    def deliver(src, row):
        dst = out_ref.at[s, row : row + src.shape[0]]
        for d in range(1, S):
            remote(src, dst, f_ssem, f_rsem, shift=lax.rem(s + d, S)).start()
        pltpu.make_async_copy(src, dst, o_sem.at[1]).start()

    for c in range(NP):
        def take(k, acc):
            return acc + r2[k, c * RP : (c + 1) * RP, :].astype(F32)

        settle(r2.at[1:, c * RP : (c + 1) * RP], r2_rsem.at[c])
        own_rows = stage[pl.ds(pl.multiple_of((c * NC + chip) * RP, 8), RP), :]
        acc = lax.fori_loop(1, NC, take, own_rows)
        fdat[c] = acc
        deliver(fdat.at[c], c * RP)
        if c == 0:
            lo, hi = pieces[c]
            base = 2 * (hi - lo)
            load = jnp.concatenate(
                [
                    acc[base + 3 * g : base + 3 * g + 1]
                    + acc[base + 3 * g + 1 : base + 3 * g + 2]
                    + acc[base + 3 * g + 2 : base + 3 * g + 3]
                    for g in range(G // LANE)
                ],
                axis=1,
            )[:, :W]
            spread = dot(load, squares, precision=HIGH)
            for l in range(L):
                fwt[l : l + 1, :] = spread[:, l * LANE : (l + 1) * LANE]
            deliver(fwt, NP * RP)

    settle(out_ref.at[: S - 1], f_rsem)
    settle(shbuf.at[: S - 1], sh_ssem)
    settle(cbuf.at[: W - 1], ag_ssem.at[0])
    settle(pbuf.at[: W - 1], ag_ssem.at[1])
    settle(r1, r1_ssem)
    settle(snd.at[: NC - 1], r2_ssem)
    settle(scr.at[: S - 1], sc_ssem)
    settle(selfr.at[: S - 1], sf_ssem)
    settle(out_ref.at[: S - 1], f_ssem)
    ev_copy.wait()
    settle(out_ref.at[:1], o_sem.at[1])


def unfold(nl, L, RP, rows_ref, ev_in, out_ref, ev_ref):
    S = rows_ref.shape[0]
    pieces = cuts(L)
    for t in range(S):
        first = min(t * L, nl - L)
        for c, (lo, hi) in enumerate(pieces):
            for l in range(lo, hi):
                n = first + l
                if n < t * L:
                    continue
                at_row = c * RP + 2 * (l - lo)
                for r, row in enumerate((at_row, at_row + 1, len(pieces) * RP + l)):
                    col = (r * nl + n) * LANE
                    out_ref[:, col : col + LANE] = rows_ref[t, row : row + 1, :]
    ev_ref[...] = ev_in[...]


def local(W, S, particles, group_id, ctf_curves, projections, inv_noise, shifts):
    R = particles.shape[0]
    coeffs = inv_noise.shape[0]
    nl = coeffs // LANE
    L = -(-nl // S)
    C = L * LANE
    NTL = shifts.shape[0]
    NT = NTL * S
    H = W // 2
    NB = H // 2
    G = padded(W, LANE)
    rows = H * NT
    qn = padded(L * NR + 1, 16)
    pieces = cuts(L)
    RP = padded(max(2 * (hi - lo) for lo, hi in pieces) + 3 * G // LANE, 16)
    NP = len(pieces)
    any_spec = pl.BlockSpec(memory_space=pl.ANY)
    vm = pl.BlockSpec(memory_space=pltpu.VMEM)
    dma = pltpu.SemaphoreType.DMA
    V = pltpu.VMEM
    out, ev = pl.pallas_call(
        functools.partial(kernel, (W, S, nl, L, NTL, R)),
        out_shape=(
            jax.ShapeDtypeStruct((S, NP * RP + padded(L, 8), LANE), F32),
            jax.ShapeDtypeStruct((1, R), F32),
        ),
        in_specs=[any_spec] * 6,
        out_specs=(any_spec, any_spec),
        scratch_shapes=[
            V((1, R), jnp.int32),
            V((2, R, C), BF16),
            V((W, 1, C), F32),
            V((W, 2, C), BF16),
            V((S, 2, NTL), jnp.int32),
            V((1, 2 * coeffs), BF16),
            V((1, coeffs), F32),
            V((NT, C), F32),
            V((NT, C), F32),
            V((R, 2 * C), BF16),
            V((2 * R, 2 * C), BF16),
            V((1, R), F32),
            V((W, C), F32),
            V((W, C), F32),
            V((H + NB, 2 * R), F32),
            V((max(S - 1, 1), H + NB, 2 * R), F32),
            V((H, 2 * R), F32),
            V((R, C), F32),
            V((rows, 2 * R), jnp.int16),
            V((max(S - 1, 1), rows, 2 * R), jnp.int16),
            V((rows, 2 * R), F32),
            V((qn, 4 * NT), BF16),
            V((2 * REACH, LANE), F32),
            V((qn * W, 2 * R), F32),
            V((W, 2 * C + G), F32),
            V((H, 2 * C + G), F32),
            V((H * NP * RP, LANE), F32),
            V((H, NP * RP, LANE), BF16),
            V((H, NP * RP, LANE), BF16),
            V((NP, RP, LANE), F32),
            V((padded(L, 8), LANE), F32),
            dma(()), dma((5,)),
            dma((2,)), dma((W // 2,)), dma(()), dma(()), dma(()),
            dma(()), dma(()), dma((max(S - 1, 1), NB + 1)),
            dma(()), dma((NP,)), dma(()), dma((NP,)),
            dma(()), dma(()), dma((2,)),
        ],
        compiler_params=pltpu.CompilerParams(
            collective_id=0, has_side_effects=True, vmem_limit_bytes=60 * 1024 * 1024
        ),
    )(
        particles, group_id.reshape(1, R), ctf_curves, projections, inv_noise, shifts.T,
    )
    out, ev = pl.pallas_call(
        functools.partial(unfold, nl, L, RP),
        out_shape=(
            jax.ShapeDtypeStruct((1, 3 * coeffs), F32),
            jax.ShapeDtypeStruct((1, R), F32),
        ),
        in_specs=[vm, vm],
        out_specs=(vm, vm),
    )(out, ev)
    return out, ev.reshape(R)


def solution(mesh):
    W, S = mesh.shape["wide"], mesh.shape["shift"]
    placed = (
        P("wide", None),
        P("wide", None),
        P("wide", None),
        P("wide", None),
        P(),
        P("shift", None),
    )
    return jax.shard_map(
        functools.partial(local, W, S), mesh=mesh, in_specs=placed,
        out_specs=(P("wide", None), P("wide")), check_vma=False,
    )
```
